32 devices in a mesh: dp: 4 (over y, x), seq: 4 (over z), head: 2 (over core).
Axes of the slice: x: 2, y: 2, z: 4, core: 2. Of those that a mesh axis runs over, the one named last changes fastest.
Arguments:
- hidden_in: bfloat16 [4, 512, 1024], P('dp', 'seq'), may hold values from -10 to 10
- out_grad: bfloat16 [4, 512, 1024], P('dp', 'seq'), may hold values from -6 to 6
- doc_ids: int32 [4, 512], P('dp'), may hold values from 0 to 3, never falling along the last dimension, each value on 1 to 256 neighbouring positions
- mixer_gain: bfloat16 [1024], P(('dp', 'seq')), may hold values from 0.5 to 1.5
- ssm_gate_proj: bfloat16 [1024, 1536], P(('dp', 'seq'), 'head'), may hold values from -0.1875 to 0.1875
- ssm_value_proj: bfloat16 [1024, 1536], P(('dp', 'seq'), 'head'), may hold values from -0.1875 to 0.1875
- ssm_bc_proj: bfloat16 [1024, 256], P(('dp', 'seq')), may hold values from -0.1875 to 0.1875
- ssm_step_proj: bfloat16 [1024, 24], P(('dp', 'seq'), 'head'), may hold values from -0.1875 to 0.1875
- conv_value_kernel: float32 [4, 1536], P(None, 'head'), may hold values from -3 to 3
- conv_value_bias: float32 [1536], P('head'), may hold values from -3 to 3
- conv_bc_kernel: float32 [4, 256], replicated, may hold values from -3 to 3
- conv_bc_bias: float32 [256], replicated, may hold values from -3 to 3
- decay_log: float32 [24], P('head'), may hold values from -13 to -3
- step_bias: float32 [24], P('head'), may hold values from -0.5 to 1
- skip_gain: float32 [24], P('head'), may hold values from 0.5 to 1.5
- ssm_norm_gain: float32 [1536], P('head'), may hold values from 0.5 to 1.5
- ssm_out_proj: bfloat16 [1536, 1024], P('head', ('dp', 'seq')), may hold values from -0.15625 to 0.15625
- query_proj: bfloat16 [1024, 512], P(('dp', 'seq'), 'head'), may hold values from -1 to 1
- key_proj: bfloat16 [1024, 128], P(('dp', 'seq'), 'head'), may hold values from -1 to 1
- value_proj: bfloat16 [1024, 128], P(('dp', 'seq'), 'head'), may hold values from -0.1875 to 0.1875
- attn_out_proj: bfloat16 [512, 1024], P('head', ('dp', 'seq')), may hold values from -1.5 to 1.5
- ffn_gain: bfloat16 [1024], P(('dp', 'seq')), may hold values from 0.5 to 1.5
- ffn_gate_proj: bfloat16 [1024, 2048], P(('dp', 'seq'), 'head'), may hold values from -0.1875 to 0.1875
- ffn_up_proj: bfloat16 [1024, 2048], P(('dp', 'seq'), 'head'), may hold values from -0.1875 to 0.1875
- ffn_down_proj: bfloat16 [2048, 1024], P('head', ('dp', 'seq')), may hold values from -0.125 to 0.125
Outputs:
- block_out: bfloat16 [4, 512, 1024], P('dp', 'seq')
- hidden_grad: float32 [4, 512, 1024], P('dp', 'seq')
- grad_mixer_gain: float32 [1024], P(('dp', 'seq'))
- grad_ssm_gate_proj: float32 [1024, 1536], P(('dp', 'seq'), 'head')
- grad_ssm_value_proj: float32 [1024, 1536], P(('dp', 'seq'), 'head')
- grad_ssm_bc_proj: float32 [1024, 256], P(('dp', 'seq'))
- grad_ssm_step_proj: float32 [1024, 24], P(('dp', 'seq'), 'head')
- grad_conv_value_kernel: float32 [4, 1536], P(None, 'head')
- grad_conv_value_bias: float32 [1536], P('head')
- grad_conv_bc_kernel: float32 [4, 256], replicated
- grad_conv_bc_bias: float32 [256], replicated
- grad_decay_log: float32 [24], P('head')
- grad_step_bias: float32 [24], P('head')
- grad_skip_gain: float32 [24], P('head')
- grad_ssm_norm_gain: float32 [1536], P('head')
- grad_ssm_out_proj: float32 [1536, 1024], P('head', ('dp', 'seq'))
- grad_query_proj: float32 [1024, 512], P(('dp', 'seq'), 'head')
- grad_key_proj: float32 [1024, 128], P(('dp', 'seq'), 'head')
- grad_value_proj: float32 [1024, 128], P(('dp', 'seq'), 'head')
- grad_attn_out_proj: float32 [512, 1024], P('head', ('dp', 'seq'))
- grad_ffn_gain: float32 [1024], P(('dp', 'seq'))
- grad_ffn_gate_proj: float32 [1024, 2048], P(('dp', 'seq'), 'head')
- grad_ffn_up_proj: float32 [1024, 2048], P(('dp', 'seq'), 'head')
- grad_ffn_down_proj: float32 [2048, 1024], P('head', ('dp', 'seq'))
The draws below stay inside these ranges and needn't reach their ends.
Inputs may be any that keep to these rules, and one draw needn't show every extreme that they name: `doc_ids`: along each sequence the ids never fall; one document holds at most 256 tokens, and some document holds exactly that many.
All inputs are finite; a program needn't handle non-finite values.
Results may differ from the reference program's by a relative error of at most 0.028.
Values may be sent and summed in bfloat16 or wider, within the bound.
No kernel may reach another device: no remote copies, remote signals or barrier semaphores. Data moves between devices by JAX's collectives and lax.ppermute only.
A program may use at most 128 MiB of HBM per device.

```python
import math
from functools import partial
import jax
import jax.numpy as jnp
import numpy as np
from jax import lax

D = 1024
MHEADS = 24
HDIM = 64
NSTATE = 128
QHEADS = 8
KVHEADS = 2
FF = 2048
KCONV = 4
DOCS = 4
SPAN = 128
DINNER = 1536
LEN = 512
SEQS = 4


def draw_decay_log(key, part):
    lower = math.log(0.3 / LEN)
    upper = math.log(1.0 / 30.0)
    return jax.random.uniform(key, (MHEADS,), jnp.float32, lower, upper)


def drawn_projection(key, salt, heads):
    noise = jax.random.normal(jax.random.fold_in(key, salt), (D, heads * HDIM), jnp.float32)
    return jnp.clip(noise, -6.0, 6.0) / math.sqrt(D)


def draw_hidden_in(key, part):
    base = jnp.clip(jax.random.normal(jax.random.fold_in(key, 1), (SEQS, LEN, D), jnp.float32), -6.0, 6.0)
    return base.astype(jnp.bfloat16)


def draw_query_proj(key, part):
    weights = drawn_projection(key, 2, QHEADS)
    return weights.astype(jnp.bfloat16)


def draw_key_proj(key, part):
    weights = drawn_projection(key, 3, KVHEADS)
    return weights.astype(jnp.bfloat16)


def block_scale(rng, dims, split, least, largest):
    factor_of, own = 1.0, jax.random.fold_in(rng, 6)
    for axis_at, shards_of in split:
        heights = jnp.exp(jax.random.uniform(jax.random.fold_in(own, axis_at), (shards_of,), jnp.float32, least / len(split), largest / len(split)))
        factor_of = factor_of * jnp.repeat(heights, dims[axis_at] // shards_of).reshape([-1 if axis == axis_at else 1 for axis in range(len(dims))])
    return factor_of


def profile(number_of, total, most, slope):
    portions = [(1 << 20) // math.isqrt(grade ** slope) + 1 for grade in range(2, number_of + 1)]
    surplus, given = total - most - (number_of - 1), [1] * (number_of - 1)
    while surplus > 0:
        movable = [i for i in range(number_of - 1) if given[i] < most]
        pool, left = sum([portions[i] for i in movable]), surplus
        for i in movable:
            addition = min(most - given[i], max(1, left * portions[i] // pool), surplus)
            given[i] = given[i] + addition
            surplus = surplus - addition
    return np.array([most] + given)


def ragged_sizes(own_key, count, total, limit, lean):
    if count == 2:
        one = jax.random.randint(own_key, (), max(1, total - limit), min(limit, total - 1) + 1)
        return jnp.stack([one, total - one])
    lengths = jnp.asarray(profile(count, total, limit, lean), jnp.int32)
    twos = (count - 1) // 2
    donor, sink = lengths[1:1 + 2 * twos:2], lengths[2:2 + 2 * twos:2]
    room = jnp.minimum(donor - 1, limit - sink)
    shifted = jax.random.randint(jax.random.fold_in(own_key, 1), (twos,), 0, 1 << 20) % (room + 1)
    lengths = lengths.at[1:1 + 2 * twos:2].set(donor - shifted).at[2:2 + 2 * twos:2].set(sink + shifted)
    return lengths[jax.random.permutation(jax.random.fold_in(own_key, 2), count)]


def gaussian(key, dims, scale, limit, shards=(), kind=jnp.bfloat16):
    drawn = scale * jax.random.normal(key, dims, jnp.float32)
    if shards:
        drawn = drawn * block_scale(key, dims, shards, -0.22, 0.18)
    return jnp.clip(drawn, -limit, limit).astype(kind)


def setup_inputs(seed: int = 0) -> dict:
    splits = jax.random.split(jax.random.key(seed), 26)
    hidden_in = draw_hidden_in(jax.random.fold_in(splits[25], 71), 0)
    out_grad = gaussian(splits[1], (SEQS, LEN, D), 1.0, 6.0, ((0, 4), (1, 4)))
    doc_ids = jax.vmap(lambda own: jnp.searchsorted(jnp.cumsum(ragged_sizes(own, DOCS, LEN, LEN // 2, 0)), jnp.arange(LEN), side="right"))(jax.random.split(splits[2], SEQS)).reshape((SEQS, LEN)).astype(jnp.int32)
    mixer_gain = jnp.clip(1.0 + 0.1 * jax.random.normal(splits[3], (D,), jnp.float32), 0.5, 1.5).astype(jnp.bfloat16)
    ssm_gate_proj = gaussian(splits[4], (D, DINNER), D ** -0.5, 0.1875, ((0, 16), (1, 2)))
    ssm_value_proj = gaussian(splits[5], (D, DINNER), D ** -0.5, 0.1875, ((0, 16), (1, 2)))
    ssm_bc_proj = gaussian(splits[6], (D, 2 * NSTATE), D ** -0.5, 0.1875, ((0, 16),))
    ssm_step_proj = gaussian(splits[7], (D, MHEADS), D ** -0.5, 0.1875, ((0, 16), (1, 2)))
    conv_value_kernel = gaussian(splits[8], (KCONV, DINNER), KCONV ** -0.5, 3.0, ((1, 2),), jnp.float32)
    conv_value_bias = gaussian(splits[9], (DINNER,), 0.5, 3.0, ((0, 2),), jnp.float32)
    conv_bc_kernel = gaussian(splits[10], (KCONV, 2 * NSTATE), KCONV ** -0.5, 3.0, (), jnp.float32)
    conv_bc_bias = gaussian(splits[11], (2 * NSTATE,), 0.5, 3.0, (), jnp.float32)
    decay_log = draw_decay_log(jax.random.fold_in(splits[25], 71), 0)
    step_bias = jnp.clip(-0.5 + 1.5 * jax.random.uniform(splits[13], (MHEADS,), jnp.float32) ** block_scale(splits[13], (MHEADS,), ((0, 2),), -0.2, 0.2), -0.5, 1.0)
    skip_gain = jnp.clip(0.5 + 1.0 * jax.random.uniform(splits[14], (MHEADS,), jnp.float32) ** block_scale(splits[14], (MHEADS,), ((0, 2),), -0.2, 0.2), 0.5, 1.5)
    ssm_norm_gain = jnp.clip(1.0 + 0.1 * jax.random.normal(splits[15], (DINNER,), jnp.float32), 0.5, 1.5)
    ssm_out_proj = gaussian(splits[16], (DINNER, D), DINNER ** -0.5, 0.15625, ((0, 2), (1, 16)))
    query_proj = draw_query_proj(jax.random.fold_in(splits[25], 71), 0)
    key_proj = draw_key_proj(jax.random.fold_in(splits[25], 71), 0)
    value_proj = gaussian(splits[19], (D, KVHEADS * HDIM), D ** -0.5, 0.1875, ((0, 16), (1, 2)))
    attn_out_proj = gaussian(splits[20], (QHEADS * HDIM, D), (max(1, QHEADS * HDIM * 16 // LEN)) ** -0.5, 1.5, ((0, 2), (1, 16)))
    ffn_gain = jnp.clip(1.0 + 0.1 * jax.random.normal(splits[21], (D,), jnp.float32), 0.5, 1.5).astype(jnp.bfloat16)
    ffn_gate_proj = gaussian(splits[22], (D, FF), D ** -0.5, 0.1875, ((0, 16), (1, 2)))
    ffn_up_proj = gaussian(splits[23], (D, FF), D ** -0.5, 0.1875, ((0, 16), (1, 2)))
    ffn_down_proj = gaussian(splits[24], (FF, D), FF ** -0.5, 0.125, ((0, 2), (1, 16)))
    return dict(hidden_in=hidden_in, out_grad=out_grad, doc_ids=doc_ids, mixer_gain=mixer_gain, ssm_gate_proj=ssm_gate_proj, ssm_value_proj=ssm_value_proj, ssm_bc_proj=ssm_bc_proj, ssm_step_proj=ssm_step_proj, conv_value_kernel=conv_value_kernel, conv_value_bias=conv_value_bias, conv_bc_kernel=conv_bc_kernel, conv_bc_bias=conv_bc_bias, decay_log=decay_log, step_bias=step_bias, skip_gain=skip_gain, ssm_norm_gain=ssm_norm_gain, ssm_out_proj=ssm_out_proj, query_proj=query_proj, key_proj=key_proj, value_proj=value_proj, attn_out_proj=attn_out_proj, ffn_gain=ffn_gain, ffn_gate_proj=ffn_gate_proj, ffn_up_proj=ffn_up_proj, ffn_down_proj=ffn_down_proj)


EPS = 1e-05
HIGH = lax.Precision.HIGHEST
ROPE_BASE = 10000.0
NEG_LARGE = -1e+30

def product(left, right):
    return jnp.dot(left, right, preferred_element_type=jnp.float32)

def round_half(values):
    return lax.optimization_barrier(values.astype(jnp.bfloat16)).astype(jnp.float32)

def rms_apply(values, gain):
    scale = lax.rsqrt(lax.optimization_barrier(jnp.mean(values * values, axis=-1, keepdims=True)) + EPS)
    normed = values * scale
    return (normed, scale, normed * gain.astype(jnp.float32))

def rms_backward(grad_out, normed, scale, gain):
    grad_normed = grad_out * gain.astype(jnp.float32)
    inner = lax.optimization_barrier(jnp.mean(grad_normed * normed, axis=-1, keepdims=True))
    leading = tuple(range(grad_out.ndim - 1))
    return (scale * (grad_normed - normed * inner), lax.optimization_barrier(jnp.sum(grad_out * normed, axis=leading)))

def rope_tables(positions, width):
    half = width // 2
    frequency = ROPE_BASE ** (-2.0 * jnp.arange(half, dtype=jnp.float32) / width)
    angles = positions.astype(jnp.float32)[:, None] * frequency[None, :]
    return (jnp.cos(angles), jnp.sin(angles))

def rotate(values, cosine, sine, sign):
    half = values.shape[-1] // 2
    first = values[..., :half]
    second = values[..., half:]
    return jnp.concatenate([first * cosine - sign * second * sine, second * cosine + sign * first * sine], axis=-1)

def doc_masks(doc_window, width):
    length = doc_window.shape[1] - width
    own = doc_window[:, width:]
    conv_mask = jnp.stack([doc_window[:, offset:offset + length] == own for offset in range(width + 1)], axis=-1).astype(jnp.float32)
    before = doc_window[:, width - 1]
    order = jnp.arange(length, dtype=jnp.int32)
    causal = order[:, None] >= order[None, :]
    same_doc = (own[:, :, None] == own[:, None, :]) & causal[None]
    live = (own == before[:, None]).astype(jnp.float32)
    tail = (own == own[:, length - 1:]).astype(jnp.float32)
    return (conv_mask, same_doc, live, tail, live[:, length - 1])

def conv_silu(padded, kernel, bias, conv_mask):
    length = conv_mask.shape[1]
    total = bias
    for offset in range(kernel.shape[0]):
        total = total + kernel[offset] * padded[:, offset:offset + length] * conv_mask[:, :, offset:offset + 1]
    return jax.nn.silu(total)

def value_inputs(value_ext, step_raw, kernel, bias, decay_log, step_bias, conv_mask):
    act_value = conv_silu(value_ext, kernel, bias, conv_mask)
    step = jax.nn.softplus(step_raw + step_bias)
    log_decay = -step * jnp.exp(decay_log)
    return (act_value, step, log_decay)

def span_ends(act_value, act_bc, step, log_decay, tail, last_live):
    batch, length, heads = step.shape
    hdim = act_value.shape[-1] // heads
    nstate = act_bc.shape[-1] // 2
    values = act_value.reshape(batch, length, heads, hdim)
    cumul = jnp.cumsum(log_decay, axis=1)
    total = cumul[:, -1]
    weights = jnp.exp(total[:, None, :] - cumul) * step * tail[..., None]
    ends = jnp.einsum('slh,slhp,sln->shpn', weights, values, act_bc[..., :nstate], precision=HIGH)
    return (ends, jnp.exp(total) * last_live[:, None])

def span_output(act_value, act_bc, step, log_decay, gate_raw, state_in, skip_gain, norm_gain, same_doc, live):
    batch, length, heads = step.shape
    hdim = act_value.shape[-1] // heads
    nstate = act_bc.shape[-1] // 2
    values = act_value.reshape(batch, length, heads, hdim)
    inputs_b = act_bc[..., :nstate]
    readout = act_bc[..., nstate:]
    cumul = jnp.cumsum(log_decay, axis=1)
    within = same_doc[..., None]
    gap = jnp.where(within, cumul[:, :, None, :] - cumul[:, None, :, :], 0.0)
    kernel = jnp.where(within, jnp.exp(gap), 0.0)
    intersection = jnp.einsum('stn,srn->str', readout, inputs_b, precision=HIGH)
    mixing = kernel * intersection[..., None] * step[:, None, :, :]
    intra = jnp.einsum('strh,srhp->sthp', mixing, values, precision=HIGH)
    carried = jnp.einsum('shpn,stn->sthp', state_in, readout, precision=HIGH) * (jnp.exp(cumul) * live[..., None])[..., None]
    output = intra + carried + skip_gain[None, None, :, None] * values
    gated = output.reshape(batch, length, heads * hdim) * jax.nn.silu(gate_raw)
    scale = lax.rsqrt(lax.optimization_barrier(jnp.mean(gated * gated, axis=-1, keepdims=True)) + EPS)
    return gated * scale * norm_gain

def mamba_sequence(value_raw, bc_raw, step_raw, gate_raw, conv_value_kernel, conv_value_bias, conv_bc_kernel, conv_bc_bias, decay_log, step_bias, skip_gain, ssm_norm_gain, documents):
    width = KCONV - 1
    count = LEN // SPAN
    value_pad = jnp.concatenate([jnp.zeros((width, value_raw.shape[1]), jnp.float32), value_raw], axis=0)
    bc_pad = jnp.concatenate([jnp.zeros((width, bc_raw.shape[1]), jnp.float32), bc_raw], axis=0)
    doc_pad = jnp.concatenate([jnp.full((width,), -1, jnp.int32), documents], axis=0)

    def advance(state, index):
        start = (index * SPAN).astype(jnp.int32)
        value_ext = lax.dynamic_slice_in_dim(value_pad, start, SPAN + width, 0)[None]
        bc_ext = lax.dynamic_slice_in_dim(bc_pad, start, SPAN + width, 0)[None]
        doc_window = lax.dynamic_slice_in_dim(doc_pad, start, SPAN + width, 0)[None]
        step_part = lax.dynamic_slice_in_dim(step_raw, start, SPAN, 0)[None]
        gate_part = lax.dynamic_slice_in_dim(gate_raw, start, SPAN, 0)[None]
        conv_mask, same_doc, live, tail, last_live = doc_masks(doc_window, width)
        act_value, step, log_decay = value_inputs(value_ext, step_part, conv_value_kernel, conv_value_bias, decay_log, step_bias, conv_mask)
        act_bc = conv_silu(bc_ext, conv_bc_kernel, conv_bc_bias, conv_mask)
        ends, decay = span_ends(act_value, act_bc, step, log_decay, tail, last_live)
        normed = span_output(act_value, act_bc, step, log_decay, gate_part, state, skip_gain, ssm_norm_gain, same_doc, live)
        return (decay[:, :, None, None] * state + ends, normed[0])
    init = jnp.zeros((1, MHEADS, HDIM, NSTATE), jnp.float32)
    _, outputs = lax.scan(advance, init, jnp.arange(count, dtype=jnp.int32))
    return outputs.reshape(LEN, MHEADS * HDIM)

def block_mask(start, block, order, documents):
    rows_pos = lax.dynamic_slice_in_dim(order, start, block, 0)
    rows_doc = lax.dynamic_slice_in_dim(documents, start, block, 0)
    return ((order[None, :] <= rows_pos[:, None]) & (documents[None, :] == rows_doc[:, None]))[None]

def attention_forward(query, keys, values, documents):
    group = QHEADS // KVHEADS
    key_full = jnp.repeat(keys, group, axis=1).astype(jnp.float32)
    value_full = jnp.repeat(values, group, axis=1).astype(jnp.float32)
    block = min(512, LEN)
    order = jnp.arange(LEN, dtype=jnp.int32)
    scale = HDIM ** (-0.5)

    def one_block(start):
        rows = lax.dynamic_slice_in_dim(query, start, block, 0).astype(jnp.float32)
        allowed = block_mask(start, block, order, documents)
        scores = jnp.einsum('qhd,khd->hqk', rows, key_full) * scale
        peak = lax.optimization_barrier(jnp.max(jnp.where(allowed, scores, NEG_LARGE), axis=-1, keepdims=True))
        total = lax.optimization_barrier(jnp.sum(jnp.where(allowed, jnp.exp(scores - peak), 0.0), axis=-1, keepdims=True))
        log_total = peak + jnp.log(total)
        probs = round_half(jnp.where(allowed, jnp.exp(scores - log_total), 0.0))
        return (jnp.einsum('hqk,khd->qhd', probs, value_full), log_total[..., 0])
    starts = jnp.arange(LEN // block, dtype=jnp.int32) * block
    outputs, logs = lax.map(one_block, starts)
    return (outputs.reshape(LEN, QHEADS, HDIM), jnp.moveaxis(logs, 0, 1).reshape(QHEADS, LEN))

def attention_reverse_pass(query, keys, values, documents, attn_out, log_total, grad_attn):
    group = QHEADS // KVHEADS
    key_full = jnp.repeat(keys, group, axis=1).astype(jnp.float32)
    value_full = jnp.repeat(values, group, axis=1).astype(jnp.float32)
    block = min(512, LEN)
    order = jnp.arange(LEN, dtype=jnp.int32)
    scale = HDIM ** (-0.5)
    delta = lax.optimization_barrier(jnp.sum(grad_attn * attn_out, axis=-1))
    grad_round = round_half(grad_attn)

    def one_block(carry, start):
        key_acc, value_acc = carry
        rows = lax.dynamic_slice_in_dim(query, start, block, 0).astype(jnp.float32)
        grads = lax.dynamic_slice_in_dim(grad_round, start, block, 0)
        deltas = jnp.transpose(lax.dynamic_slice_in_dim(delta, start, block, 0))
        logs = lax.dynamic_slice_in_dim(log_total, start, block, 1)
        allowed = block_mask(start, block, order, documents)
        scores = jnp.einsum('qhd,khd->hqk', rows, key_full) * scale
        probs = jnp.where(allowed, jnp.exp(scores - logs[..., None]), 0.0)
        value_acc = value_acc + jnp.einsum('hqk,qhd->khd', round_half(probs), grads)
        grad_probs = jnp.einsum('qhd,khd->hqk', grads, value_full)
        score_gradients = round_half(probs * (grad_probs - deltas[..., None]) * scale)
        key_acc = key_acc + jnp.einsum('hqk,qhd->khd', score_gradients, rows)
        return ((key_acc, value_acc), jnp.einsum('hqk,khd->qhd', score_gradients, key_full))
    zeros = jnp.zeros((LEN, QHEADS, HDIM), jnp.float32)
    starts = jnp.arange(LEN // block, dtype=jnp.int32) * block
    (key_acc, value_acc), grad_rows = lax.scan(one_block, (zeros, zeros), starts)
    grad_query = grad_rows.reshape(LEN, QHEADS, HDIM)
    grad_keys = lax.optimization_barrier(jnp.sum(key_acc.reshape(LEN, KVHEADS, group, HDIM), axis=2))
    grad_values = lax.optimization_barrier(jnp.sum(value_acc.reshape(LEN, KVHEADS, group, HDIM), axis=2))
    return (grad_query, grad_keys, grad_values)

def one_sequence(hidden, upstream, documents, weights):
    mixer_gain, ssm_gate_proj, ssm_value_proj, ssm_bc_proj, ssm_step_proj, conv_value_kernel, conv_value_bias, conv_bc_kernel, conv_bc_bias, decay_log, step_bias, skip_gain, ssm_norm_gain, ssm_out_proj, query_proj, key_proj, value_proj, attn_out_proj, ffn_gain, ffn_gate_proj, ffn_up_proj, ffn_down_proj = weights
    resid = hidden.astype(jnp.float32)
    normed_pre, scale_pre, scaled_pre = rms_apply(resid, mixer_gain)
    mixer_in = scaled_pre.astype(jnp.bfloat16)
    gate_raw = product(mixer_in, ssm_gate_proj)
    value_raw = product(mixer_in, ssm_value_proj)
    bc_raw = product(mixer_in, ssm_bc_proj)
    step_raw = product(mixer_in, ssm_step_proj)
    ssm_normed, ssm_pull = jax.vjp(partial(mamba_sequence, documents=documents), value_raw, bc_raw, step_raw, gate_raw, conv_value_kernel, conv_value_bias, conv_bc_kernel, conv_bc_bias, decay_log, step_bias, skip_gain, ssm_norm_gain)
    ssm_in = ssm_normed.astype(jnp.bfloat16)
    positions = jnp.arange(LEN, dtype=jnp.int32)
    cosine, sine = rope_tables(positions, HDIM)
    cosine = cosine[:, None, :]
    sine = sine[:, None, :]
    query = rotate(product(mixer_in, query_proj).reshape(LEN, QHEADS, HDIM), cosine, sine, 1.0).astype(jnp.bfloat16)
    keys = rotate(product(mixer_in, key_proj).reshape(LEN, KVHEADS, HDIM), cosine, sine, 1.0).astype(jnp.bfloat16)
    values = product(mixer_in, value_proj).reshape(LEN, KVHEADS, HDIM).astype(jnp.bfloat16)
    attn_out, log_total = attention_forward(query, keys, values, documents)
    attn_in = attn_out.reshape(LEN, QHEADS * HDIM).astype(jnp.bfloat16)
    mixed = resid + (product(ssm_in, ssm_out_proj) + product(attn_in, attn_out_proj))
    normed_ffn, scale_ffn, scaled_ffn = rms_apply(mixed, ffn_gain)
    feedforward_input = scaled_ffn.astype(jnp.bfloat16)
    gate = product(feedforward_input, ffn_gate_proj)
    upward = product(feedforward_input, ffn_up_proj)
    sigma = jax.nn.sigmoid(gate)
    hidden_act = (gate * sigma * upward).astype(jnp.bfloat16)
    block_out = (mixed + product(hidden_act, ffn_down_proj)).astype(jnp.bfloat16)
    grad_ffn_down = product(hidden_act.T, upstream)
    grad_hidden = product(upstream, ffn_down_proj.T)
    grad_gate_pre = (grad_hidden * upward * sigma * (1.0 + gate * (1.0 - sigma))).astype(jnp.bfloat16)
    grad_up_pre = (grad_hidden * gate * sigma).astype(jnp.bfloat16)
    grad_ffn_gate = product(feedforward_input.T, grad_gate_pre)
    grad_ffn_up = product(feedforward_input.T, grad_up_pre)
    grad_ffn_in = product(grad_gate_pre, ffn_gate_proj.T) + product(grad_up_pre, ffn_up_proj.T)
    grad_mixed_norm, grad_ffn_gain = rms_backward(grad_ffn_in, normed_ffn, scale_ffn, ffn_gain)
    grad_mixed = upstream.astype(jnp.float32) + grad_mixed_norm
    branch_gradient = grad_mixed.astype(jnp.bfloat16)
    grad_ssm_out = product(ssm_in.T, branch_gradient)
    grad_attn_out = product(attn_in.T, branch_gradient)
    grad_ssm_in = product(branch_gradient, ssm_out_proj.T)
    grad_attn = product(branch_gradient, attn_out_proj.T).reshape(LEN, QHEADS, HDIM)
    grad_query, grad_keys, grad_values = attention_reverse_pass(query, keys, values, documents, attn_out, log_total, grad_attn)
    grad_query_in = rotate(grad_query, cosine, sine, -1.0).reshape(LEN, QHEADS * HDIM).astype(jnp.bfloat16)
    grad_keys_in = rotate(grad_keys, cosine, sine, -1.0).reshape(LEN, KVHEADS * HDIM).astype(jnp.bfloat16)
    grad_values_in = grad_values.reshape(LEN, KVHEADS * HDIM).astype(jnp.bfloat16)
    grad_value_raw, grad_bc_raw, grad_step_raw, grad_gate_raw, grad_kernel_value, grad_bias_value, grad_kernel_bc, grad_bias_bc, grad_decay_log, grad_step_bias, grad_skip, grad_norm_gain = ssm_pull(grad_ssm_in)
    grad_gate_in = grad_gate_raw.astype(jnp.bfloat16)
    grad_value_in = grad_value_raw.astype(jnp.bfloat16)
    grad_bc_in = grad_bc_raw.astype(jnp.bfloat16)
    grad_step_in = grad_step_raw.astype(jnp.bfloat16)
    grad_mixer_in = product(grad_gate_in, ssm_gate_proj.T) + product(grad_value_in, ssm_value_proj.T) + product(grad_bc_in, ssm_bc_proj.T) + product(grad_step_in, ssm_step_proj.T) + product(grad_query_in, query_proj.T) + product(grad_keys_in, key_proj.T) + product(grad_values_in, value_proj.T)
    grad_pre_norm, grad_mixer_gain = rms_backward(grad_mixer_in, normed_pre, scale_pre, mixer_gain)
    hidden_grad = grad_mixed + grad_pre_norm
    grads = (grad_mixer_gain, product(mixer_in.T, grad_gate_in), product(mixer_in.T, grad_value_in), product(mixer_in.T, grad_bc_in), product(mixer_in.T, grad_step_in), grad_kernel_value, grad_bias_value, grad_kernel_bc, grad_bias_bc, grad_decay_log, grad_step_bias, grad_skip, grad_norm_gain, grad_ssm_out, product(mixer_in.T, grad_query_in), product(mixer_in.T, grad_keys_in), product(mixer_in.T, grad_values_in), grad_attn_out, grad_ffn_gain, grad_ffn_gate, grad_ffn_up, grad_ffn_down)
    return (block_out, hidden_grad, grads)

def reference(hidden_in, out_grad, doc_ids, mixer_gain, ssm_gate_proj, ssm_value_proj, ssm_bc_proj, ssm_step_proj, conv_value_kernel, conv_value_bias, conv_bc_kernel, conv_bc_bias, decay_log, step_bias, skip_gain, ssm_norm_gain, ssm_out_proj, query_proj, key_proj, value_proj, attn_out_proj, ffn_gain, ffn_gate_proj, ffn_up_proj, ffn_down_proj):
    weights = (mixer_gain, ssm_gate_proj, ssm_value_proj, ssm_bc_proj, ssm_step_proj, conv_value_kernel, conv_value_bias, conv_bc_kernel, conv_bc_bias, decay_log, step_bias, skip_gain, ssm_norm_gain, ssm_out_proj, query_proj, key_proj, value_proj, attn_out_proj, ffn_gain, ffn_gate_proj, ffn_up_proj, ffn_down_proj)
    zeros = tuple((jnp.zeros(weight.shape, jnp.float32) for weight in weights))

    def per_sequence(carry, inputs):
        hidden, upstream, documents = inputs
        block_out, hidden_grad, grads = one_sequence(hidden, upstream, documents, weights)
        return (tuple((left + right for left, right in zip(carry, grads))), (block_out, hidden_grad))
    totals, outputs = lax.scan(per_sequence, zeros, (hidden_in, out_grad, doc_ids))
    return (outputs[0], outputs[1], totals[0], totals[1], totals[2], totals[3], totals[4], totals[5], totals[6], totals[7], totals[8], totals[9], totals[10], totals[11], totals[12], totals[13], totals[14], totals[15], totals[16], totals[17], totals[18], totals[19], totals[20], totals[21])
```

```python
from functools import partial

import jax
import jax.numpy as jnp
from jax import lax
from jax.sharding import PartitionSpec as P

HDIM = 64


EPS = 1e-05
HIGH = lax.Precision.HIGHEST
ROPE_BASE = 10000.0
NEG_LARGE = -1e30


def passed_along(block, axis, distance):
    devices = range(lax.axis_size(axis))
    route = [(i - distance, i) for i in devices if i - distance in devices]
    return lax.ppermute(block, axis, route)


def prefix_2(value, axis, join, neutral, backward):
    count, mine = (lax.axis_size(axis), lax.axis_index(axis))
    pieces = jax.tree.map(lambda part: lax.all_gather(part, axis), value)
    if backward:
        pieces = jax.tree.map(lambda part: part[::-1], pieces)
        mine = count - 1 - mine
    total = jax.tree.map(
        lambda part, zero: jnp.full_like(part, 0) + jnp.asarray(zero, part.dtype), value, neutral
    )

    def turn(position, total):
        longer = join(total, jax.tree.map(lambda part: part[position], pieces))
        return jax.tree.map(lambda new, old: jnp.where(position < mine, new, old), longer, total)

    return lax.fori_loop(0, count - 1, turn, total)


def matmul(left, right):
    return jnp.dot(left, right, preferred_element_type=jnp.float32)


def back_product(gradient_term, weight):
    return jnp.einsum("slo,io->sli", gradient_term, weight, preferred_element_type=jnp.float32)


def weight_grad(activation_list, gradient_term):
    return jnp.einsum(
        "yux,yup->xp", activation_list, gradient_term, preferred_element_type=jnp.float32
    )


def rms_apply(values, gain):
    scale = lax.rsqrt(jnp.mean(values * values, axis=-1, keepdims=True) + EPS)
    normed = values * scale
    return (normed, scale, normed * gain.astype(jnp.float32))


def rms_backward(grad_out, normed, scale, gain):
    grad_normed = grad_out * gain.astype(jnp.float32)
    inner = jnp.mean(grad_normed * normed, axis=-1, keepdims=True)
    leading = tuple(range(grad_out.ndim - 1))
    return (scale * (grad_normed - normed * inner), jnp.sum(grad_out * normed, axis=leading))


def rope_tables(positions, width):
    half = width // 2
    frequency = ROPE_BASE ** (-2.0 * jnp.arange(half, dtype=jnp.float32) / width)
    angles = positions.astype(jnp.float32)[:, None] * frequency[None, :]
    return (jnp.cos(angles), jnp.sin(angles))


def rotate(values, cosine, sine, sign):
    half = values.shape[-1] // 2
    first = values[..., :half]
    second = values[..., half:]
    return jnp.concatenate(
        [first * cosine - sign * second * sine, second * cosine + sign * first * sine], axis=-1
    )


def doc_masks(doc_window, width):
    length = doc_window.shape[1] - width
    own = doc_window[:, width:]
    conv_mask = jnp.stack(
        [doc_window[:, offset : offset + length] == own for offset in range(width + 1)], axis=-1
    ).astype(jnp.float32)
    before = doc_window[:, width - 1]
    order = jnp.arange(length, dtype=jnp.int32)
    causal = order[:, None] >= order[None, :]
    same_doc = (own[:, :, None] == own[:, None, :]) & causal[None]
    live = (own == before[:, None]).astype(jnp.float32)
    tail = (own == own[:, length - 1 :]).astype(jnp.float32)
    return (conv_mask, same_doc, live, tail, live[:, length - 1])


def conv_silu(padded, kernel, bias, conv_mask):
    length = conv_mask.shape[1]
    total = bias
    for offset in range(kernel.shape[0]):
        total = (
            total
            + kernel[offset]
            * padded[:, offset : offset + length]
            * conv_mask[:, :, offset : offset + 1]
        )
    return jax.nn.silu(total)


def value_inputs(value_ext, step_raw, kernel, bias, decay_log, step_bias, conv_mask):
    act_value = conv_silu(value_ext, kernel, bias, conv_mask)
    step = jax.nn.softplus(step_raw + step_bias)
    log_decay = -step * jnp.exp(decay_log)
    return (act_value, step, log_decay)


def span_ends(act_value, act_bc, step, log_decay, tail, last_live):
    batch, length, heads = step.shape
    hdim = act_value.shape[-1] // heads
    nstate = act_bc.shape[-1] // 2
    values = act_value.reshape(batch, length, heads, hdim)
    cumul = jnp.cumsum(log_decay, axis=1)
    total = cumul[:, -1]
    weights = jnp.exp(total[:, None, :] - cumul) * step * tail[..., None]
    ends = jnp.einsum("slh,slhp,sln->shpn", weights, values, act_bc[..., :nstate], precision=HIGH)
    return (ends, jnp.exp(total) * last_live[:, None])


def span_gated(act_value, act_bc, step, log_decay, gate_raw, state_in, skip_gain, same_doc, live):
    batch, length, heads = step.shape
    hdim = act_value.shape[-1] // heads
    nstate = act_bc.shape[-1] // 2
    values = act_value.reshape(batch, length, heads, hdim)
    inputs_b = act_bc[..., :nstate]
    readout = act_bc[..., nstate:]
    cumul = jnp.cumsum(log_decay, axis=1)
    within = same_doc[..., None]
    gap = jnp.where(within, cumul[:, :, None, :] - cumul[:, None, :, :], 0.0)
    kernel = jnp.where(within, jnp.exp(gap), 0.0)
    intersection = jnp.einsum("stn,srn->str", readout, inputs_b, precision=HIGH)
    mixing = kernel * intersection[..., None] * step[:, None, :, :]
    intra = jnp.einsum("strh,srhp->sthp", mixing, values, precision=HIGH)
    carried = (
        jnp.einsum("shpn,stn->sthp", state_in, readout, precision=HIGH)
        * (jnp.exp(cumul) * live[..., None])[..., None]
    )
    output = intra + carried + skip_gain[None, None, :, None] * values
    return output.reshape(batch, length, heads * hdim) * jax.nn.silu(gate_raw)


def combine_states(earlier, later):
    return (earlier[0] * later[0], earlier[1] * later[0][:, :, None, None] + later[1])


def head_sum(values):
    return lax.psum(values, "head")


def norm_share(values):
    return lax.psum(values, "head")


def key_block():
    return 512


def block_scores(query_group, key_value_rows, block_start, block, doc_ids, query_pos, query_doc):
    batch, length, key_heads, group, hdim = query_group.shape
    piece = lax.dynamic_slice_in_dim(key_value_rows, block_start, block, 1)
    split = key_heads * hdim
    keys = piece[..., :split].reshape(batch, block, key_heads, hdim)
    values = piece[..., split:].reshape(batch, block, key_heads, hdim)
    scores = jnp.einsum(
        "sqcgd,skcd->scgqk", query_group, keys, preferred_element_type=jnp.float32
    ) * hdim ** (-0.5)
    key_pos = block_start + jnp.arange(block, dtype=jnp.int32)
    key_doc = lax.dynamic_slice_in_dim(doc_ids, block_start, block, 1)
    allowed = (key_pos[None, None, :] <= query_pos[None, :, None]) & (
        key_doc[:, None, :] == query_doc[:, :, None]
    )
    return (scores, allowed[:, None, None], keys, values)


def local(
    hidden_in,
    out_grad,
    doc_ids,
    mixer_gain,
    ssm_gate_proj,
    ssm_value_proj,
    ssm_bc_proj,
    ssm_step_proj,
    conv_value_kernel,
    conv_value_bias,
    conv_bc_kernel,
    conv_bc_bias,
    decay_log,
    step_bias,
    skip_gain,
    ssm_norm_gain,
    ssm_out_proj,
    query_proj,
    key_proj,
    value_proj,
    attn_out_proj,
    ffn_gain,
    ffn_gate_proj,
    ffn_up_proj,
    ffn_down_proj,
):
    batch, length, width = hidden_in.shape
    fetched = (
        lax.all_gather(mixer_gain, ("dp", "seq"), axis=0, tiled=True),
        lax.all_gather(ssm_gate_proj, ("dp", "seq"), axis=0, tiled=True),
        lax.all_gather(ssm_value_proj, ("dp", "seq"), axis=0, tiled=True),
        lax.all_gather(ssm_bc_proj, ("dp", "seq"), axis=0, tiled=True),
        lax.all_gather(ssm_step_proj, ("dp", "seq"), axis=0, tiled=True),
        lax.all_gather(query_proj, ("dp", "seq"), axis=0, tiled=True),
        lax.all_gather(key_proj, ("dp", "seq"), axis=0, tiled=True),
        lax.all_gather(value_proj, ("dp", "seq"), axis=0, tiled=True),
        lax.all_gather(ffn_gain, ("dp", "seq"), axis=0, tiled=True),
        lax.all_gather(ffn_gate_proj, ("dp", "seq"), axis=0, tiled=True),
        lax.all_gather(ffn_up_proj, ("dp", "seq"), axis=0, tiled=True),
        lax.all_gather(ssm_out_proj, ("dp", "seq"), axis=1, tiled=True),
        lax.all_gather(attn_out_proj, ("dp", "seq"), axis=1, tiled=True),
        lax.all_gather(ffn_down_proj, ("dp", "seq"), axis=1, tiled=True),
    )
    (
        full_mixer_gain,
        full_gate_proj,
        full_value_proj,
        full_bc_proj,
        full_step_proj,
        full_query_proj,
        full_key_proj,
        full_attn_value,
        full_ffn_gain,
        full_ffn_gate,
        full_ffn_up,
        full_ssm_out,
        full_attn_out,
        full_ffn_down,
    ) = fetched
    start = lax.axis_index("seq") * length
    conv_width = conv_value_kernel.shape[0] - 1
    query_heads = full_query_proj.shape[1] // HDIM
    key_heads = full_key_proj.shape[1] // HDIM
    group = query_heads // key_heads
    resid = hidden_in.astype(jnp.float32)
    normed_pre, scale_pre, scaled_pre = rms_apply(resid, full_mixer_gain)
    mixer_in = scaled_pre.astype(jnp.bfloat16)
    gate_raw = matmul(mixer_in, full_gate_proj)
    value_raw = matmul(mixer_in, full_value_proj)
    bc_raw = matmul(mixer_in, full_bc_proj)
    step_raw = matmul(mixer_in, full_step_proj)
    doc_pad = jnp.concatenate([jnp.full((batch, conv_width), -1, jnp.int32), doc_ids], axis=1)
    doc_window = lax.dynamic_slice_in_dim(doc_pad, start, length + conv_width, 1)
    conv_mask, same_doc, live, tail, last_live = doc_masks(doc_window, conv_width)
    edges = passed_along(
        (value_raw[:, length - conv_width :], bc_raw[:, length - conv_width :]), "seq", 1
    )
    value_ext = jnp.concatenate([edges[0], value_raw], axis=1)
    bc_ext = jnp.concatenate([edges[1], bc_raw], axis=1)
    (act_value, step, log_decay), value_pull = jax.vjp(
        partial(value_inputs, conv_mask=conv_mask),
        value_ext,
        step_raw,
        conv_value_kernel,
        conv_value_bias,
        decay_log,
        step_bias,
    )
    act_bc, bc_pull = jax.vjp(
        partial(conv_silu, conv_mask=conv_mask), bc_ext, conv_bc_kernel, conv_bc_bias
    )
    (ends, decay), ends_pull = jax.vjp(
        partial(span_ends, tail=tail, last_live=last_live), act_value, act_bc, step, log_decay
    )
    prefix = prefix_2(
        (decay, ends), "seq", combine_states, (jnp.ones_like(decay), jnp.zeros_like(ends)), False
    )
    state_in = prefix[1]
    gated, gated_pull = jax.vjp(
        partial(span_gated, same_doc=same_doc, live=live),
        act_value,
        act_bc,
        step,
        log_decay,
        gate_raw,
        state_in,
        skip_gain,
    )
    inner_width = gated.shape[-1] * lax.axis_size("head")
    square_sum = norm_share(jnp.sum(gated * gated, axis=-1))
    norm_scale = lax.rsqrt(square_sum[..., None] / inner_width + EPS)
    gated_normed = gated * norm_scale
    ssm_in = (gated_normed * ssm_norm_gain).astype(jnp.bfloat16)
    positions = start + jnp.arange(length, dtype=jnp.int32)
    cosine, sine = rope_tables(positions, HDIM)
    cosine = cosine[None, :, None, :]
    sine = sine[None, :, None, :]
    query = rotate(
        matmul(mixer_in, full_query_proj).reshape(batch, length, query_heads, HDIM),
        cosine,
        sine,
        1.0,
    ).astype(jnp.bfloat16)
    keys_new = rotate(
        matmul(mixer_in, full_key_proj).reshape(batch, length, key_heads, HDIM), cosine, sine, 1.0
    ).astype(jnp.bfloat16)
    values_new = matmul(mixer_in, full_attn_value).astype(jnp.bfloat16)
    kv_local = jnp.concatenate(
        [keys_new.reshape(batch, length, key_heads * HDIM), values_new], axis=-1
    )
    key_value_rows = lax.all_gather(kv_local, "seq", axis=1, tiled=True)
    query_group = query.reshape(batch, length, key_heads, group, HDIM)
    query_doc = lax.dynamic_slice_in_dim(doc_ids, start, length, 1)
    block = key_block()
    block_count = (start + length - 1) // block + 1

    def stats_step(index, carry):
        peak, total = carry
        scores, allowed, _, _ = block_scores(
            query_group, key_value_rows, index * block, block, doc_ids, positions, query_doc
        )
        masked = jnp.where(allowed, scores, NEG_LARGE)
        new_peak = jnp.maximum(peak, jnp.max(masked, axis=-1))
        total = total * jnp.exp(peak - new_peak) + jnp.sum(
            jnp.where(allowed, jnp.exp(masked - new_peak[..., None]), 0.0), axis=-1
        )
        return (new_peak, total)

    stat_shape = (batch, key_heads, group, length)
    peak, total = lax.fori_loop(
        0,
        block_count,
        stats_step,
        (jnp.full(stat_shape, NEG_LARGE, jnp.float32), jnp.zeros(stat_shape, jnp.float32)),
    )
    log_total = peak + jnp.log(total)

    def value_step(index, accum):
        scores, allowed, _, values = block_scores(
            query_group, key_value_rows, index * block, block, doc_ids, positions, query_doc
        )
        probs = jnp.where(allowed, jnp.exp(scores - log_total[..., None]), 0.0).astype(jnp.bfloat16)
        return accum + jnp.einsum(
            "scgqk,skcd->sqcgd", probs, values, preferred_element_type=jnp.float32
        )

    attn_out = lax.fori_loop(0, block_count, value_step, jnp.zeros(query_group.shape, jnp.float32))
    attn_in = attn_out.reshape(batch, length, query_heads * HDIM).astype(jnp.bfloat16)
    mixed = resid + head_sum(matmul(ssm_in, full_ssm_out) + matmul(attn_in, full_attn_out))
    normed_ffn, scale_ffn, scaled_ffn = rms_apply(mixed, full_ffn_gain)
    feedforward_input = scaled_ffn.astype(jnp.bfloat16)
    gate = matmul(feedforward_input, full_ffn_gate)
    upward = matmul(feedforward_input, full_ffn_up)
    sigma = jax.nn.sigmoid(gate)
    hidden_act = (gate * sigma * upward).astype(jnp.bfloat16)
    block_out = (mixed + head_sum(matmul(hidden_act, full_ffn_down))).astype(jnp.bfloat16)
    fetched = (
        lax.all_gather(mixer_gain, ("dp", "seq"), axis=0, tiled=True),
        lax.all_gather(ssm_gate_proj, ("dp", "seq"), axis=0, tiled=True),
        lax.all_gather(ssm_value_proj, ("dp", "seq"), axis=0, tiled=True),
        lax.all_gather(ssm_bc_proj, ("dp", "seq"), axis=0, tiled=True),
        lax.all_gather(ssm_step_proj, ("dp", "seq"), axis=0, tiled=True),
        lax.all_gather(query_proj, ("dp", "seq"), axis=0, tiled=True),
        lax.all_gather(key_proj, ("dp", "seq"), axis=0, tiled=True),
        lax.all_gather(value_proj, ("dp", "seq"), axis=0, tiled=True),
        lax.all_gather(ffn_gain, ("dp", "seq"), axis=0, tiled=True),
        lax.all_gather(ffn_gate_proj, ("dp", "seq"), axis=0, tiled=True),
        lax.all_gather(ffn_up_proj, ("dp", "seq"), axis=0, tiled=True),
        lax.all_gather(ssm_out_proj, ("dp", "seq"), axis=1, tiled=True),
        lax.all_gather(attn_out_proj, ("dp", "seq"), axis=1, tiled=True),
        lax.all_gather(ffn_down_proj, ("dp", "seq"), axis=1, tiled=True),
    )
    (
        full_mixer_gain,
        full_gate_proj,
        full_value_proj,
        full_bc_proj,
        full_step_proj,
        full_query_proj,
        full_key_proj,
        full_attn_value,
        full_ffn_gain,
        full_ffn_gate,
        full_ffn_up,
        full_ssm_out,
        full_attn_out,
        full_ffn_down,
    ) = fetched
    grad_top = out_grad.astype(jnp.float32)
    grad_ffn_down = weight_grad(hidden_act, out_grad)
    grad_hidden = back_product(out_grad, full_ffn_down)
    grad_gate_pre = (grad_hidden * upward * sigma * (1.0 + gate * (1.0 - sigma))).astype(
        jnp.bfloat16
    )
    grad_up_pre = (grad_hidden * gate * sigma).astype(jnp.bfloat16)
    grad_ffn_gate = weight_grad(feedforward_input, grad_gate_pre)
    grad_ffn_up = weight_grad(feedforward_input, grad_up_pre)
    grad_ffn_in = head_sum(
        back_product(grad_gate_pre, full_ffn_gate) + back_product(grad_up_pre, full_ffn_up)
    )
    grad_mixed_norm, grad_ffn_gain = rms_backward(grad_ffn_in, normed_ffn, scale_ffn, full_ffn_gain)
    grad_mixed = grad_top + grad_mixed_norm
    branch_gradient = grad_mixed.astype(jnp.bfloat16)
    grad_ssm_out = weight_grad(ssm_in, branch_gradient)
    grad_attn_out = weight_grad(attn_in, branch_gradient)
    grad_ssm = back_product(branch_gradient, full_ssm_out)
    grad_attn = back_product(branch_gradient, full_attn_out).reshape(
        batch, length, key_heads, group, HDIM
    )
    delta = jnp.transpose(jnp.sum(grad_attn * attn_out, axis=-1), (0, 2, 3, 1))
    grad_round = grad_attn.astype(jnp.bfloat16)

    def back_step(index, carry):
        grad_query, grad_kv = carry
        block_start = index * block
        scores, allowed, keys, values = block_scores(
            query_group, key_value_rows, block_start, block, doc_ids, positions, query_doc
        )
        probs = jnp.where(allowed, jnp.exp(scores - log_total[..., None]), 0.0)
        grad_values = jnp.einsum(
            "scgqk,sqcgd->skcd",
            probs.astype(jnp.bfloat16),
            grad_round,
            preferred_element_type=jnp.float32,
        )
        grad_probs = jnp.einsum(
            "sqcgd,skcd->scgqk", grad_round, values, preferred_element_type=jnp.float32
        )
        score_gradients = (probs * (grad_probs - delta[..., None]) * HDIM ** (-0.5)).astype(
            jnp.bfloat16
        )
        grad_query = grad_query + jnp.einsum(
            "scgqk,skcd->sqcgd", score_gradients, keys, preferred_element_type=jnp.float32
        )
        grad_keys = jnp.einsum(
            "scgqk,sqcgd->skcd", score_gradients, query_group, preferred_element_type=jnp.float32
        )
        piece = jnp.concatenate(
            [
                grad_keys.reshape(batch, block, key_heads * HDIM),
                grad_values.reshape(batch, block, key_heads * HDIM),
            ],
            axis=-1,
        )
        return (grad_query, lax.dynamic_update_slice_in_dim(grad_kv, piece, block_start, 1))

    grad_query, grad_kv = lax.fori_loop(
        0,
        block_count,
        back_step,
        (jnp.zeros(query_group.shape, jnp.float32), jnp.zeros(key_value_rows.shape, jnp.float32)),
    )
    grad_kv_own = lax.psum_scatter(grad_kv, "seq", scatter_dimension=1, tiled=True)
    grad_query_in = (
        rotate(grad_query.reshape(batch, length, query_heads, HDIM), cosine, sine, -1.0)
        .reshape(batch, length, query_heads * HDIM)
        .astype(jnp.bfloat16)
    )
    grad_key_in = (
        rotate(
            grad_kv_own[..., : key_heads * HDIM].reshape(batch, length, key_heads, HDIM),
            cosine,
            sine,
            -1.0,
        )
        .reshape(batch, length, key_heads * HDIM)
        .astype(jnp.bfloat16)
    )
    grad_value_in = grad_kv_own[..., key_heads * HDIM :].astype(jnp.bfloat16)
    grad_norm_gain = jnp.sum(grad_ssm * gated_normed, axis=(0, 1))
    scaled_grad = grad_ssm * ssm_norm_gain
    inner = norm_share(jnp.sum(scaled_grad * gated_normed, axis=-1))
    grad_gated = norm_scale * (scaled_grad - gated_normed * (inner[..., None] / inner_width))
    (
        grad_act_value,
        grad_act_bc,
        grad_step,
        grad_log_decay,
        grad_gate_raw,
        grad_state_in,
        grad_skip,
    ) = gated_pull(grad_gated)
    suffix = prefix_2(
        (decay, grad_state_in),
        "seq",
        combine_states,
        (jnp.ones_like(decay), jnp.zeros_like(grad_state_in)),
        True,
    )
    grad_ends = suffix[1]
    grad_decay = jnp.sum(grad_ends * state_in, axis=(2, 3))
    extra_value, extra_bc, extra_step, extra_log = ends_pull((grad_ends, grad_decay))
    (
        grad_value_ext,
        grad_step_raw,
        grad_kernel_value,
        grad_bias_value,
        grad_decay_log,
        grad_step_bias,
    ) = value_pull(
        (grad_act_value + extra_value, grad_step + extra_step, grad_log_decay + extra_log)
    )
    grad_bc_ext, grad_kernel_bc, grad_bias_bc = bc_pull(head_sum(grad_act_bc + extra_bc))
    boundary_gradients = passed_along(
        (grad_value_ext[:, :conv_width], grad_bc_ext[:, :conv_width]), "seq", -1
    )
    grad_value_raw = (
        grad_value_ext[:, conv_width:].at[:, length - conv_width :].add(boundary_gradients[0])
    )
    grad_bc_raw = (
        grad_bc_ext[:, conv_width:].at[:, length - conv_width :].add(boundary_gradients[1])
    )
    grad_gate_in = grad_gate_raw.astype(jnp.bfloat16)
    grad_value_ssm = grad_value_raw.astype(jnp.bfloat16)
    grad_bc_in = grad_bc_raw.astype(jnp.bfloat16)
    grad_step_in = grad_step_raw.astype(jnp.bfloat16)
    partial_sum = (
        back_product(grad_gate_in, full_gate_proj)
        + back_product(grad_value_ssm, full_value_proj)
        + back_product(grad_step_in, full_step_proj)
        + back_product(grad_query_in, full_query_proj)
        + back_product(grad_key_in, full_key_proj)
        + back_product(grad_value_in, full_attn_value)
    )
    grad_mixer_in = head_sum(partial_sum) + back_product(grad_bc_in, full_bc_proj)
    grad_pre_norm, grad_mixer_gain = rms_backward(
        grad_mixer_in, normed_pre, scale_pre, full_mixer_gain
    )
    hidden_grad = grad_mixed + grad_pre_norm
    reduced = (
        lax.psum_scatter(grad_mixer_gain, ("dp", "seq"), scatter_dimension=0, tiled=True),
        lax.psum_scatter(
            weight_grad(mixer_in, grad_gate_in), ("dp", "seq"), scatter_dimension=0, tiled=True
        ),
        lax.psum_scatter(
            weight_grad(mixer_in, grad_value_ssm), ("dp", "seq"), scatter_dimension=0, tiled=True
        ),
        lax.psum_scatter(
            weight_grad(mixer_in, grad_bc_in), ("dp", "seq"), scatter_dimension=0, tiled=True
        ),
        lax.psum_scatter(
            weight_grad(mixer_in, grad_step_in), ("dp", "seq"), scatter_dimension=0, tiled=True
        ),
        lax.psum_scatter(
            weight_grad(mixer_in, grad_query_in), ("dp", "seq"), scatter_dimension=0, tiled=True
        ),
        lax.psum_scatter(
            weight_grad(mixer_in, grad_key_in), ("dp", "seq"), scatter_dimension=0, tiled=True
        ),
        lax.psum_scatter(
            weight_grad(mixer_in, grad_value_in), ("dp", "seq"), scatter_dimension=0, tiled=True
        ),
        lax.psum_scatter(grad_ffn_gain, ("dp", "seq"), scatter_dimension=0, tiled=True),
        lax.psum_scatter(grad_ffn_gate, ("dp", "seq"), scatter_dimension=0, tiled=True),
        lax.psum_scatter(grad_ffn_up, ("dp", "seq"), scatter_dimension=0, tiled=True),
        lax.psum_scatter(grad_ssm_out, ("dp", "seq"), scatter_dimension=1, tiled=True),
        lax.psum_scatter(grad_attn_out, ("dp", "seq"), scatter_dimension=1, tiled=True),
        lax.psum_scatter(grad_ffn_down, ("dp", "seq"), scatter_dimension=1, tiled=True),
    )
    small = lax.psum(
        (
            grad_kernel_value,
            grad_bias_value,
            grad_kernel_bc,
            grad_bias_bc,
            grad_decay_log,
            grad_step_bias,
            grad_skip,
            grad_norm_gain,
        ),
        ("dp", "seq"),
    )
    return (
        block_out,
        hidden_grad,
        reduced[0],
        reduced[1],
        reduced[2],
        reduced[3],
        reduced[4],
        small[0],
        small[1],
        small[2],
        small[3],
        small[4],
        small[5],
        small[6],
        small[7],
        reduced[11],
        reduced[5],
        reduced[6],
        reduced[7],
        reduced[12],
        reduced[8],
        reduced[9],
        reduced[10],
        reduced[13],
    )


def shift_pairs(count, step):
    return [(i, (i + step) % count) for i in range(count)]


def from_ahead(block, axis, step):
    count = lax.axis_size(axis)
    return lax.ppermute(block, axis, shift_pairs(count, -step % count))


def to_ahead(block, axis, step):
    return lax.ppermute(block, axis, shift_pairs(lax.axis_size(axis), step))


def partner(block):
    return to_ahead(block, "head", 1)


def wrap_slice(block, start, axis):
    size = block.shape[axis]
    return lax.dynamic_slice_in_dim(jnp.concatenate([block, block], axis=axis), start, size, axis)


def dot_bf(left, right, dims):
    return lax.dot_general(
        left.astype(jnp.bfloat16),
        right.astype(jnp.bfloat16),
        (dims, ((), ())),
        preferred_element_type=jnp.float32,
    )


def gather_tokens(half, heads_at):
    seqs = lax.axis_size("seq")
    own = jnp.stack([half] + [from_ahead(half, "seq", j) for j in range(1, seqs)])
    other = partner(own)
    pair = jnp.where(
        heads_at == 0, jnp.stack([own, other], axis=1), jnp.stack([other, own], axis=1)
    )
    return pair.reshape(-1, half.shape[-1])


def reduce_tokens(left, weight, heads_at):
    seqs, heads = (lax.axis_size("seq"), lax.axis_size("head"))
    split = left.reshape(seqs, heads, -1, left.shape[-1])
    half = split.shape[2]
    theirs = lax.dynamic_index_in_dim(split, 1 - heads_at, 1, keepdims=False)
    mine = lax.dynamic_index_in_dim(split, heads_at, 1, keepdims=False)
    sent = dot_bf(theirs.reshape(seqs * half, -1), weight, ((1,), (1,))).astype(jnp.bfloat16)
    got = partner(sent).astype(jnp.float32)
    both = dot_bf(mine.reshape(seqs * half, -1), weight, ((1,), (1,))) + got
    both = both.reshape(seqs, half, -1)
    total = both[0]
    for j in range(1, seqs):
        total = total + to_ahead(both[j].astype(jnp.bfloat16), "seq", j).astype(jnp.float32)
    return total


def sum_tokens(values):
    seqs = lax.axis_size("seq")
    values = values + partner(values)
    block = values.shape[0] // seqs
    total = values
    for j in range(1, seqs):
        total = total + jnp.roll(from_ahead(values, "seq", j), j * block, axis=0)
    return total


def both_halves(half, heads_at):
    other = partner(half)
    return jnp.where(
        heads_at == 0,
        jnp.concatenate([half, other], axis=0),
        jnp.concatenate([other, half], axis=0),
    )


def spread_weights(pieces):
    rows = lax.all_to_all(pieces, "seq", 0, 0, tiled=True)
    own = rows.reshape(-1, rows.shape[-1])
    return jnp.concatenate(
        [own] + [from_ahead(own, "dp", k) for k in range(1, lax.axis_size("dp"))], axis=0
    )


def collect_weight_grad(activation, gradient, seq_at):
    count, seqs = (lax.axis_size("dp"), lax.axis_size("seq"))
    chunk = activation.shape[1] // count
    total = None
    for k in list(range(1, count)) + [0]:
        part = dot_bf(activation[:, k * chunk : (k + 1) * chunk], gradient, ((0,), (0,)))
        if k:
            part = to_ahead(part.astype(jnp.bfloat16), "dp", k).astype(jnp.float32)
        total = part if total is None else total + part
    rows = total.astype(jnp.bfloat16).reshape(seqs, chunk // seqs, -1)
    found = []
    for j in range(seqs):
        piece = lax.dynamic_index_in_dim(rows, (seq_at - j) % seqs, 0, keepdims=False)
        found.append(from_ahead(piece, "seq", j) if j else piece)
    return wrap_slice(jnp.stack(found), (seqs - seq_at) % seqs, 0).astype(jnp.float32)


def laid_out(found, first, width):
    part = jnp.moveaxis(found[:, :, first : first + width], 0, 1)
    return part.reshape(part.shape[0], -1)


def sum_all(values):
    for axis in ("dp", "seq"):
        count = lax.axis_size(axis)
        step = 1
        while step < count:
            values = values + lax.ppermute(values, axis, [(i, i ^ step) for i in range(count)])
            step *= 2
    return values


def fits_whole_sequences(mesh_sizes, batch, length, parts):
    dps, seqs, heads = mesh_sizes
    powers = all(size & (size - 1) == 0 for size in mesh_sizes)
    even = all(part % seqs == 0 for part in parts)
    return powers and even and heads == 2 and batch == 1 and length * seqs <= 1024


def whole_sequences(
    hidden_in,
    out_grad,
    doc_ids,
    mixer_gain,
    ssm_gate_proj,
    ssm_value_proj,
    ssm_bc_proj,
    ssm_step_proj,
    conv_value_kernel,
    conv_value_bias,
    conv_bc_kernel,
    conv_bc_bias,
    decay_log,
    step_bias,
    skip_gain,
    ssm_norm_gain,
    ssm_out_proj,
    query_proj,
    key_proj,
    value_proj,
    attn_out_proj,
    ffn_gain,
    ffn_gate_proj,
    ffn_up_proj,
    ffn_down_proj,
):
    bf16, f32 = (jnp.bfloat16, jnp.float32)
    dps, seqs, heads = (lax.axis_size(axis) for axis in ("dp", "seq", "head"))
    dp_at, seq_at, head_at = (lax.axis_index(axis) for axis in ("dp", "seq", "head"))
    _, length, width = hidden_in.shape
    tokens = length * seqs
    half = length // heads
    rows = ssm_gate_proj.shape[0]
    chunk = width // dps
    inner = ssm_gate_proj.shape[1] // seqs
    mheads = decay_log.shape[0] // seqs
    hdim = inner // mheads
    attn = query_proj.shape[1] // seqs
    group = attn // HDIM
    kv = key_proj.shape[1]
    bc = ssm_bc_proj.shape[1]
    nstate = bc // 2
    steps = ssm_step_proj.shape[1]
    units = ffn_gate_proj.shape[1] // seqs
    inner_width = inner * seqs * heads

    def rotated(block):
        return wrap_slice(block, dp_at * chunk, block.ndim - 1)

    def unrotated(block):
        return wrap_slice(block, (dps - dp_at) % dps * chunk, block.ndim - 1)

    def cut(block):
        return jnp.moveaxis(block.reshape(rows, seqs, -1), 1, 0)

    def same(block):
        return jnp.broadcast_to(block[None], (seqs,) + block.shape)

    def own_part(block):
        size = block.shape[-1] // seqs
        return lax.dynamic_slice_in_dim(block, seq_at * size, size, block.ndim - 1)

    hidden_half = rotated(lax.dynamic_slice_in_dim(hidden_in[0], head_at * half, half, 0))
    grad_half = rotated(lax.dynamic_slice_in_dim(out_grad[0], head_at * half, half, 0))
    hidden = gather_tokens(hidden_half, head_at).astype(f32)
    gains = lax.all_gather(
        jnp.stack([mixer_gain, ffn_gain]), ("dp", "seq"), axis=1, tiled=True
    )
    gains = rotated(gains)
    used = 2 * inner + bc + attn + 2 * kv + steps
    padding = -used % 128
    first_pieces = jnp.concatenate(
        [
            cut(ssm_gate_proj),
            cut(ssm_value_proj),
            same(ssm_bc_proj),
            cut(query_proj),
            same(key_proj),
            same(value_proj),
            same(ssm_step_proj),
            jnp.zeros((seqs, rows, padding), bf16),
        ],
        axis=-1,
    )
    weight_in = spread_weights(first_pieces)
    second_pieces = jnp.concatenate(
        [
            cut(ssm_out_proj.T),
            cut(attn_out_proj.T),
            cut(ffn_gate_proj),
            cut(ffn_up_proj),
            cut(ffn_down_proj.T),
        ],
        axis=-1,
    )
    weight_rest = spread_weights(second_pieces)
    at_out = inner + attn
    weight_out = weight_rest[:, :at_out]
    weight_ffn = weight_rest[:, at_out : at_out + 2 * units]
    weight_down = weight_rest[:, at_out + 2 * units :]

    order = jnp.arange(tokens, dtype=jnp.int32)
    positions = (order + seq_at * length) % tokens
    docs = wrap_slice(doc_ids[0], seq_at * length, 0)
    allowed = (positions[:, None] >= positions[None, :]) & (docs[:, None] == docs[None, :])
    allowed_f32 = allowed.astype(f32)

    def rms(values, gain):
        scale = lax.rsqrt(jnp.mean(values * values, axis=-1, keepdims=True) + EPS)
        normed = values * scale
        return (normed, scale, (normed * gain.astype(f32)).astype(bf16))

    _, _, mixer_in = rms(hidden, gains[0])
    raw = dot_bf(mixer_in, weight_in, ((1,), (0,)))
    at_conv = inner
    at_query = at_conv + inner + bc
    at_key = at_query + attn
    at_value = at_key + kv
    at_step = at_value + kv

    gate_raw = raw[:, :inner]
    conv_raw = raw[:, at_conv:at_query]
    taps = conv_value_kernel.shape[0]
    kernel = jnp.concatenate([own_part(conv_value_kernel), conv_bc_kernel], axis=-1)
    bias = jnp.concatenate([own_part(conv_value_bias), conv_bc_bias], axis=-1)
    masks = []
    for k in range(taps):
        shift = taps - 1 - k
        masks.append(((positions >= shift) & (jnp.roll(docs, shift) == docs)).astype(f32)[:, None])
    pre = bias
    for k in range(taps):
        pre = pre + kernel[k] * jnp.roll(conv_raw, taps - 1 - k, axis=0) * masks[k]
    pre_sigma = jax.nn.sigmoid(pre)
    act = pre * pre_sigma
    act_value = act[:, :inner]
    input_b = act[:, inner : inner + nstate].astype(bf16)
    readout = act[:, inner + nstate :].astype(bf16)

    step_raw = own_part(raw[:, at_step : at_step + steps])
    step_pre = step_raw + own_part(step_bias)
    step = jax.nn.softplus(step_pre)
    rate = jnp.exp(own_part(decay_log))
    log_decay = -step * rate
    cumul = jnp.dot(allowed_f32, log_decay, precision=HIGH)
    cumul_row = cumul.T

    def per_channel(values):
        return jnp.repeat(values, hdim, axis=-1)

    def head_sums(values):
        return jnp.sum(values.reshape(tokens, mheads, hdim), axis=-1)

    skip = per_channel(own_part(skip_gain)[None])
    stepped = (act_value * per_channel(step)).astype(bf16)
    intersection = dot_bf(readout, input_b, ((1,), (1,)))

    def decay_of(j):
        gap = jnp.where(allowed, cumul[:, j : j + 1] - cumul_row[j : j + 1, :], 0.0)
        return jnp.where(allowed, jnp.exp(gap), 0.0)

    def columns(values, j):
        return values[:, j * hdim : (j + 1) * hdim]

    mixing = [(decay_of(j) * intersection).astype(bf16) for j in range(mheads)]
    intra = jnp.concatenate(
        [dot_bf(mixing[j], columns(stepped, j), ((1,), (0,))) for j in range(mheads)], axis=-1
    )
    ssm_y = intra + skip * act_value
    gate_sigma = jax.nn.sigmoid(gate_raw)
    gate_act = gate_raw * gate_sigma
    gated = ssm_y * gate_act
    square_sum = sum_tokens(jnp.sum(gated * gated, axis=-1, keepdims=True))
    norm_scale = lax.rsqrt(square_sum / inner_width + EPS)
    gated_normed = gated * norm_scale
    norm_gain = own_part(ssm_norm_gain)
    ssm_in = (gated_normed * norm_gain).astype(bf16)

    cosine, sine = rope_tables(positions, HDIM)

    def turned(values, sign):
        return jnp.concatenate(
            [
                rotate(values[:, i * HDIM : (i + 1) * HDIM], cosine, sine, sign)
                for i in range(values.shape[1] // HDIM)
            ],
            axis=-1,
        )

    query = turned(raw[:, at_query:at_key], 1.0).astype(bf16)
    keys = turned(raw[:, at_key:at_value], 1.0).astype(bf16)
    values = raw[:, at_value:at_step].astype(bf16)
    scores_scale = HDIM ** (-0.5)
    probs, attn_out = ([], [])
    for i in range(group):
        scores = dot_bf(columns(query, i), keys, ((1,), (1,))) * scores_scale
        masked = jnp.where(allowed, scores, NEG_LARGE)
        peak = jnp.max(masked, axis=-1, keepdims=True)
        total = jnp.sum(jnp.where(allowed, jnp.exp(masked - peak), 0.0), axis=-1, keepdims=True)
        log_total = peak + jnp.log(total)
        probs.append(jnp.where(allowed, jnp.exp(scores - log_total), 0.0))
        attn_out.append(dot_bf(probs[i], values, ((1,), (0,))))
    attn_out = jnp.concatenate(attn_out, axis=-1)

    branch_in = jnp.concatenate([ssm_in, attn_out.astype(bf16)], axis=-1)
    mixed = hidden_half.astype(f32) + reduce_tokens(branch_in, weight_out, head_at)
    normed_ffn, scale_ffn, ffn_half = rms(mixed, gains[1])
    upstream = gather_tokens(grad_half, head_at)
    ffn_in = gather_tokens(ffn_half, head_at)
    both = dot_bf(ffn_in, weight_ffn, ((1,), (0,)))
    gate = both[:, :units]
    upward = both[:, units:]
    sigma = jax.nn.sigmoid(gate)
    hidden_act = (gate * sigma * upward).astype(bf16)
    grad_hidden = dot_bf(upstream, weight_down, ((1,), (0,)))
    grad_ffn = jnp.concatenate(
        [
            grad_hidden * upward * sigma * (1.0 + gate * (1.0 - sigma)),
            grad_hidden * gate * sigma,
        ],
        axis=-1,
    ).astype(bf16)

    def rms_pull(gradient, normed, scale, gain):
        scaled = gradient * gain.astype(f32)
        mean = jnp.mean(scaled * normed, axis=-1, keepdims=True)
        return (scale * (scaled - normed * mean), jnp.sum(gradient * normed, axis=0))

    grad_ffn_in = reduce_tokens(grad_ffn, weight_ffn, head_at)
    pulled, grad_ffn_gain = rms_pull(grad_ffn_in, normed_ffn, scale_ffn, gains[1])
    grad_mixed = grad_half.astype(f32) + pulled
    branch = gather_tokens(grad_mixed.astype(bf16), head_at)
    block_half = mixed + reduce_tokens(hidden_act, weight_down, head_at)
    block_out = unrotated(both_halves(block_half.astype(bf16), head_at))[None]

    grad_branch = dot_bf(branch, weight_out, ((1,), (0,)))
    grad_ssm = grad_branch[:, :inner]
    grad_attn = grad_branch[:, inner:]
    found_ffn = collect_weight_grad(ffn_in, grad_ffn, seq_at)
    found_back = jnp.concatenate(
        [
            collect_weight_grad(upstream, hidden_act, seq_at),
            collect_weight_grad(branch, branch_in, seq_at),
        ],
        axis=-1,
    )

    grad_norm_gain = jnp.sum(grad_ssm * gated_normed, axis=0)
    scaled_grad = grad_ssm * norm_gain
    overlap = sum_tokens(jnp.sum(scaled_grad * gated_normed, axis=-1, keepdims=True))

    grad_query, grad_keys, grad_values = ([], 0.0, 0.0)
    for i in range(group):
        gradient = columns(grad_attn, i)
        delta = jnp.sum(gradient * columns(attn_out, i), axis=-1, keepdims=True)
        gradient = gradient.astype(bf16)
        grad_values = grad_values + dot_bf(probs[i], gradient, ((0,), (0,)))
        grad_probs = dot_bf(gradient, values, ((1,), (1,)))
        grad_scores = (probs[i] * (grad_probs - delta) * scores_scale).astype(bf16)
        grad_query.append(dot_bf(grad_scores, keys, ((1,), (0,))))
        grad_keys = grad_keys + dot_bf(grad_scores, columns(query, i), ((0,), (0,)))
    grad_query = turned(jnp.concatenate(grad_query, axis=-1), -1.0)
    grad_keys = turned(grad_keys, -1.0)

    grad_gated = norm_scale * (scaled_grad - gated_normed * (overlap / inner_width))
    grad_y = grad_gated * gate_act
    grad_gate_raw = grad_gated * ssm_y * gate_sigma * (1.0 + gate_raw * (1.0 - gate_sigma))
    grad_y_round = grad_y.astype(bf16)
    grad_stepped, grad_intersection = ([], 0.0)
    for j in range(mheads):
        grad_stepped.append(dot_bf(mixing[j], columns(grad_y_round, j), ((0,), (0,))))
        grad_mixing = dot_bf(columns(grad_y_round, j), columns(stepped, j), ((1,), (1,)))
        grad_intersection = grad_intersection + grad_mixing * decay_of(j)
    grad_stepped = jnp.concatenate(grad_stepped, axis=-1)
    grad_intersection = grad_intersection.astype(bf16)
    grad_readout = dot_bf(grad_intersection, input_b, ((1,), (0,)))
    grad_input_b = dot_bf(grad_intersection, readout, ((0,), (0,)))
    grad_cumul = head_sums(grad_y_round.astype(f32) * intra - grad_stepped * stepped.astype(f32))
    grad_log_decay = lax.dot_general(
        allowed_f32, grad_cumul, (((0,), (0,)), ((), ())), precision=HIGH
    )
    grad_step = head_sums(grad_stepped * act_value) - grad_log_decay * rate
    grad_decay_log = jnp.sum(grad_log_decay * log_decay, axis=0)
    grad_step_raw = grad_step * jax.nn.sigmoid(step_pre)
    grad_step_bias = jnp.sum(grad_step_raw, axis=0)
    grad_skip = jnp.sum(head_sums(grad_y * act_value), axis=0)
    grad_act = jnp.concatenate(
        [grad_stepped * per_channel(step) + skip * grad_y, grad_input_b, grad_readout], axis=-1
    )
    grad_pre = grad_act * pre_sigma * (1.0 + pre * (1.0 - pre_sigma))
    grad_bias = jnp.sum(grad_pre, axis=0)
    grad_kernel, grad_conv_raw = ([], 0.0)
    for k in range(taps):
        shift = taps - 1 - k
        masked = grad_pre * masks[k]
        grad_kernel.append(jnp.sum(masked * jnp.roll(conv_raw, shift, axis=0), axis=0))
        grad_conv_raw = grad_conv_raw + jnp.roll(kernel[k] * masked, -shift, axis=0)
    grad_kernel = jnp.stack(grad_kernel)

    def in_place(block, axis):
        size = block.shape[axis]
        shape = list(block.shape)
        shape[axis] = size * seqs
        return lax.dynamic_update_slice_in_dim(
            jnp.zeros(shape, f32), block.astype(f32), seq_at * size, axis
        )

    grad_raw = jnp.concatenate(
        [
            grad_gate_raw,
            grad_conv_raw,
            grad_query,
            grad_keys,
            grad_values,
            in_place(grad_step_raw, 1),
            jnp.zeros((tokens, padding), f32),
        ],
        axis=-1,
    ).astype(bf16)
    grad_mixer_in = reduce_tokens(grad_raw, weight_in, head_at)
    normed_pre, scale_pre, _ = rms(hidden_half.astype(f32), gains[0])
    pulled, grad_mixer_gain = rms_pull(grad_mixer_in, normed_pre, scale_pre, gains[0])
    hidden_grad = unrotated(both_halves(grad_mixed + pulled, head_at))[None]
    found_in = collect_weight_grad(mixer_in, grad_raw, seq_at)

    per_half = [
        in_place(grad_kernel[:, :inner], 1).reshape(-1),
        in_place(grad_bias[:inner], 0),
        in_place(grad_norm_gain, 0),
        in_place(grad_decay_log, 0),
        in_place(grad_step_bias, 0),
        in_place(grad_skip, 0),
    ]
    whole = [
        grad_kernel[:, inner:].reshape(-1),
        grad_bias[inner:],
        unrotated(grad_mixer_gain),
        unrotated(grad_ffn_gain),
    ]

    def apart(packed, like):
        found, at = ([], 0)
        for part in like:
            found.append(packed[at : at + part.shape[0]])
            at += part.shape[0]
        return found

    packed = sum_all(jnp.concatenate(per_half + whole))
    at_whole = sum(part.shape[0] for part in per_half)
    small = apart(packed[:at_whole], per_half)
    shared = packed[at_whole:]
    shared = apart(shared + partner(shared), whole)
    grad_gains = [
        lax.dynamic_slice_in_dim(part, (dp_at * seqs + seq_at) * rows, rows, 0)
        for part in shared[2:]
    ]

    summed = jnp.sum(found_in, axis=0)
    grad_bc_proj = summed[:, at_conv + inner : at_query]
    grad_bc_proj = grad_bc_proj + partner(grad_bc_proj)
    return (
        block_out,
        hidden_grad,
        grad_gains[0],
        laid_out(found_in, 0, inner),
        laid_out(found_in, at_conv, inner),
        grad_bc_proj,
        summed[:, at_step : at_step + steps],
        small[0].reshape(taps, -1),
        small[1],
        shared[0].reshape(taps, -1),
        shared[1],
        small[3],
        small[4],
        small[5],
        small[2],
        laid_out(found_back, units, inner).T,
        laid_out(found_in, at_query, attn),
        summed[:, at_key:at_value],
        summed[:, at_value:at_step],
        laid_out(found_back, units + inner, attn).T,
        grad_gains[1],
        laid_out(found_ffn, 0, units),
        laid_out(found_ffn, units, units),
        laid_out(found_back, 0, units).T,
    )


def block_step(*args):
    hidden_in, conv_value_kernel, decay_log = (args[0], args[8], args[12])
    batch, length, _ = hidden_in.shape
    sizes = tuple(lax.axis_size(axis) for axis in ("dp", "seq", "head"))
    columns = (
        decay_log.shape[0],
        args[17].shape[1] // HDIM,
        args[22].shape[1],
        conv_value_kernel.shape[1],
    )
    if fits_whole_sequences(sizes, batch, length, columns) and args[18].shape[1] == HDIM:
        return whole_sequences(*args)
    return local(*args)


def solution(mesh):
    placed = (
        P("dp", "seq", None),
        P("dp", "seq", None),
        P("dp", None),
        P(("dp", "seq")),
        P(("dp", "seq"), "head"),
        P(("dp", "seq"), "head"),
        P(("dp", "seq"), None),
        P(("dp", "seq"), "head"),
        P(None, "head"),
        P("head"),
        P(),
        P(),
        P("head"),
        P("head"),
        P("head"),
        P("head"),
        P("head", ("dp", "seq")),
        P(("dp", "seq"), "head"),
        P(("dp", "seq"), "head"),
        P(("dp", "seq"), "head"),
        P("head", ("dp", "seq")),
        P(("dp", "seq")),
        P(("dp", "seq"), "head"),
        P(("dp", "seq"), "head"),
        P("head", ("dp", "seq")),
    )
    return jax.shard_map(
        block_step,
        mesh=mesh,
        in_specs=placed,
        out_specs=(
            P("dp", "seq", None),
            P("dp", "seq", None),
            P(("dp", "seq")),
            P(("dp", "seq"), "head"),
            P(("dp", "seq"), "head"),
            P(("dp", "seq"), None),
            P(("dp", "seq"), "head"),
            P(None, "head"),
            P("head"),
            P(),
            P(),
            P("head"),
            P("head"),
            P("head"),
            P("head"),
            P("head", ("dp", "seq")),
            P(("dp", "seq"), "head"),
            P(("dp", "seq"), "head"),
            P(("dp", "seq"), "head"),
            P("head", ("dp", "seq")),
            P(("dp", "seq")),
            P(("dp", "seq"), "head"),
            P(("dp", "seq"), "head"),
            P("head", ("dp", "seq")),
        ),
        check_vma=False,
    )
```

```python
from functools import partial

import jax
import jax.numpy as jnp
from jax import lax
from jax.experimental import pallas as pl
from jax.experimental.pallas import tpu as pltpu
from jax.sharding import PartitionSpec as P

HDIM = 64


EPS = 1e-05
HIGH = lax.Precision.HIGHEST
ROPE_BASE = 10000.0
NEG_LARGE = -1e30


def passed_along(block, axis, distance):
    devices = range(lax.axis_size(axis))
    route = [(i - distance, i) for i in devices if i - distance in devices]
    return lax.ppermute(block, axis, route)


def prefix_2(value, axis, join, neutral, backward):
    count, mine = (lax.axis_size(axis), lax.axis_index(axis))
    pieces = jax.tree.map(lambda part: lax.all_gather(part, axis), value)
    if backward:
        pieces = jax.tree.map(lambda part: part[::-1], pieces)
        mine = count - 1 - mine
    total = jax.tree.map(
        lambda part, zero: jnp.full_like(part, 0) + jnp.asarray(zero, part.dtype), value, neutral
    )

    def turn(position, total):
        longer = join(total, jax.tree.map(lambda part: part[position], pieces))
        return jax.tree.map(lambda new, old: jnp.where(position < mine, new, old), longer, total)

    return lax.fori_loop(0, count - 1, turn, total)


def matmul(left, right):
    return jnp.dot(left, right, preferred_element_type=jnp.float32)


def back_product(gradient_term, weight):
    return jnp.einsum("slo,io->sli", gradient_term, weight, preferred_element_type=jnp.float32)


def weight_grad(activation_list, gradient_term):
    return jnp.einsum(
        "yux,yup->xp", activation_list, gradient_term, preferred_element_type=jnp.float32
    )


def rms_apply(values, gain):
    scale = lax.rsqrt(jnp.mean(values * values, axis=-1, keepdims=True) + EPS)
    normed = values * scale
    return (normed, scale, normed * gain.astype(jnp.float32))


def rms_backward(grad_out, normed, scale, gain):
    grad_normed = grad_out * gain.astype(jnp.float32)
    inner = jnp.mean(grad_normed * normed, axis=-1, keepdims=True)
    leading = tuple(range(grad_out.ndim - 1))
    return (scale * (grad_normed - normed * inner), jnp.sum(grad_out * normed, axis=leading))


def rope_tables(positions, width):
    half = width // 2
    frequency = ROPE_BASE ** (-2.0 * jnp.arange(half, dtype=jnp.float32) / width)
    angles = positions.astype(jnp.float32)[:, None] * frequency[None, :]
    return (jnp.cos(angles), jnp.sin(angles))


def rotate(values, cosine, sine, sign):
    half = values.shape[-1] // 2
    first = values[..., :half]
    second = values[..., half:]
    return jnp.concatenate(
        [first * cosine - sign * second * sine, second * cosine + sign * first * sine], axis=-1
    )


def doc_masks(doc_window, width):
    length = doc_window.shape[1] - width
    own = doc_window[:, width:]
    conv_mask = jnp.stack(
        [doc_window[:, offset : offset + length] == own for offset in range(width + 1)], axis=-1
    ).astype(jnp.float32)
    before = doc_window[:, width - 1]
    order = jnp.arange(length, dtype=jnp.int32)
    causal = order[:, None] >= order[None, :]
    same_doc = (own[:, :, None] == own[:, None, :]) & causal[None]
    live = (own == before[:, None]).astype(jnp.float32)
    tail = (own == own[:, length - 1 :]).astype(jnp.float32)
    return (conv_mask, same_doc, live, tail, live[:, length - 1])


def conv_silu(padded, kernel, bias, conv_mask):
    length = conv_mask.shape[1]
    total = bias
    for offset in range(kernel.shape[0]):
        total = (
            total
            + kernel[offset]
            * padded[:, offset : offset + length]
            * conv_mask[:, :, offset : offset + 1]
        )
    return jax.nn.silu(total)


def value_inputs(value_ext, step_raw, kernel, bias, decay_log, step_bias, conv_mask):
    act_value = conv_silu(value_ext, kernel, bias, conv_mask)
    step = jax.nn.softplus(step_raw + step_bias)
    log_decay = -step * jnp.exp(decay_log)
    return (act_value, step, log_decay)


def span_ends(act_value, act_bc, step, log_decay, tail, last_live):
    batch, length, heads = step.shape
    hdim = act_value.shape[-1] // heads
    nstate = act_bc.shape[-1] // 2
    values = act_value.reshape(batch, length, heads, hdim)
    cumul = jnp.cumsum(log_decay, axis=1)
    total = cumul[:, -1]
    weights = jnp.exp(total[:, None, :] - cumul) * step * tail[..., None]
    ends = jnp.einsum("slh,slhp,sln->shpn", weights, values, act_bc[..., :nstate], precision=HIGH)
    return (ends, jnp.exp(total) * last_live[:, None])


def span_gated(act_value, act_bc, step, log_decay, gate_raw, state_in, skip_gain, same_doc, live):
    batch, length, heads = step.shape
    hdim = act_value.shape[-1] // heads
    nstate = act_bc.shape[-1] // 2
    values = act_value.reshape(batch, length, heads, hdim)
    inputs_b = act_bc[..., :nstate]
    readout = act_bc[..., nstate:]
    cumul = jnp.cumsum(log_decay, axis=1)
    within = same_doc[..., None]
    gap = jnp.where(within, cumul[:, :, None, :] - cumul[:, None, :, :], 0.0)
    kernel = jnp.where(within, jnp.exp(gap), 0.0)
    intersection = jnp.einsum("stn,srn->str", readout, inputs_b, precision=HIGH)
    mixing = kernel * intersection[..., None] * step[:, None, :, :]
    intra = jnp.einsum("strh,srhp->sthp", mixing, values, precision=HIGH)
    carried = (
        jnp.einsum("shpn,stn->sthp", state_in, readout, precision=HIGH)
        * (jnp.exp(cumul) * live[..., None])[..., None]
    )
    output = intra + carried + skip_gain[None, None, :, None] * values
    return output.reshape(batch, length, heads * hdim) * jax.nn.silu(gate_raw)


def combine_states(earlier, later):
    return (earlier[0] * later[0], earlier[1] * later[0][:, :, None, None] + later[1])


def head_sum(values):
    return lax.psum(values, "head")


def norm_share(values):
    return lax.psum(values, "head")


def key_block():
    return 512


def block_scores(query_group, key_value_rows, block_start, block, doc_ids, query_pos, query_doc):
    batch, length, key_heads, group, hdim = query_group.shape
    piece = lax.dynamic_slice_in_dim(key_value_rows, block_start, block, 1)
    split = key_heads * hdim
    keys = piece[..., :split].reshape(batch, block, key_heads, hdim)
    values = piece[..., split:].reshape(batch, block, key_heads, hdim)
    scores = jnp.einsum(
        "sqcgd,skcd->scgqk", query_group, keys, preferred_element_type=jnp.float32
    ) * hdim ** (-0.5)
    key_pos = block_start + jnp.arange(block, dtype=jnp.int32)
    key_doc = lax.dynamic_slice_in_dim(doc_ids, block_start, block, 1)
    allowed = (key_pos[None, None, :] <= query_pos[None, :, None]) & (
        key_doc[:, None, :] == query_doc[:, :, None]
    )
    return (scores, allowed[:, None, None], keys, values)


def local(
    hidden_in,
    out_grad,
    doc_ids,
    mixer_gain,
    ssm_gate_proj,
    ssm_value_proj,
    ssm_bc_proj,
    ssm_step_proj,
    conv_value_kernel,
    conv_value_bias,
    conv_bc_kernel,
    conv_bc_bias,
    decay_log,
    step_bias,
    skip_gain,
    ssm_norm_gain,
    ssm_out_proj,
    query_proj,
    key_proj,
    value_proj,
    attn_out_proj,
    ffn_gain,
    ffn_gate_proj,
    ffn_up_proj,
    ffn_down_proj,
):
    batch, length, width = hidden_in.shape
    fetched = (
        lax.all_gather(mixer_gain, ("dp", "seq"), axis=0, tiled=True),
        lax.all_gather(ssm_gate_proj, ("dp", "seq"), axis=0, tiled=True),
        lax.all_gather(ssm_value_proj, ("dp", "seq"), axis=0, tiled=True),
        lax.all_gather(ssm_bc_proj, ("dp", "seq"), axis=0, tiled=True),
        lax.all_gather(ssm_step_proj, ("dp", "seq"), axis=0, tiled=True),
        lax.all_gather(query_proj, ("dp", "seq"), axis=0, tiled=True),
        lax.all_gather(key_proj, ("dp", "seq"), axis=0, tiled=True),
        lax.all_gather(value_proj, ("dp", "seq"), axis=0, tiled=True),
        lax.all_gather(ffn_gain, ("dp", "seq"), axis=0, tiled=True),
        lax.all_gather(ffn_gate_proj, ("dp", "seq"), axis=0, tiled=True),
        lax.all_gather(ffn_up_proj, ("dp", "seq"), axis=0, tiled=True),
        lax.all_gather(ssm_out_proj, ("dp", "seq"), axis=1, tiled=True),
        lax.all_gather(attn_out_proj, ("dp", "seq"), axis=1, tiled=True),
        lax.all_gather(ffn_down_proj, ("dp", "seq"), axis=1, tiled=True),
    )
    (
        full_mixer_gain,
        full_gate_proj,
        full_value_proj,
        full_bc_proj,
        full_step_proj,
        full_query_proj,
        full_key_proj,
        full_attn_value,
        full_ffn_gain,
        full_ffn_gate,
        full_ffn_up,
        full_ssm_out,
        full_attn_out,
        full_ffn_down,
    ) = fetched
    start = lax.axis_index("seq") * length
    conv_width = conv_value_kernel.shape[0] - 1
    query_heads = full_query_proj.shape[1] // HDIM
    key_heads = full_key_proj.shape[1] // HDIM
    group = query_heads // key_heads
    resid = hidden_in.astype(jnp.float32)
    normed_pre, scale_pre, scaled_pre = rms_apply(resid, full_mixer_gain)
    mixer_in = scaled_pre.astype(jnp.bfloat16)
    gate_raw = matmul(mixer_in, full_gate_proj)
    value_raw = matmul(mixer_in, full_value_proj)
    bc_raw = matmul(mixer_in, full_bc_proj)
    step_raw = matmul(mixer_in, full_step_proj)
    doc_pad = jnp.concatenate([jnp.full((batch, conv_width), -1, jnp.int32), doc_ids], axis=1)
    doc_window = lax.dynamic_slice_in_dim(doc_pad, start, length + conv_width, 1)
    conv_mask, same_doc, live, tail, last_live = doc_masks(doc_window, conv_width)
    edges = passed_along(
        (value_raw[:, length - conv_width :], bc_raw[:, length - conv_width :]), "seq", 1
    )
    value_ext = jnp.concatenate([edges[0], value_raw], axis=1)
    bc_ext = jnp.concatenate([edges[1], bc_raw], axis=1)
    (act_value, step, log_decay), value_pull = jax.vjp(
        partial(value_inputs, conv_mask=conv_mask),
        value_ext,
        step_raw,
        conv_value_kernel,
        conv_value_bias,
        decay_log,
        step_bias,
    )
    act_bc, bc_pull = jax.vjp(
        partial(conv_silu, conv_mask=conv_mask), bc_ext, conv_bc_kernel, conv_bc_bias
    )
    (ends, decay), ends_pull = jax.vjp(
        partial(span_ends, tail=tail, last_live=last_live), act_value, act_bc, step, log_decay
    )
    prefix = prefix_2(
        (decay, ends), "seq", combine_states, (jnp.ones_like(decay), jnp.zeros_like(ends)), False
    )
    state_in = prefix[1]
    gated, gated_pull = jax.vjp(
        partial(span_gated, same_doc=same_doc, live=live),
        act_value,
        act_bc,
        step,
        log_decay,
        gate_raw,
        state_in,
        skip_gain,
    )
    inner_width = gated.shape[-1] * lax.axis_size("head")
    square_sum = norm_share(jnp.sum(gated * gated, axis=-1))
    norm_scale = lax.rsqrt(square_sum[..., None] / inner_width + EPS)
    gated_normed = gated * norm_scale
    ssm_in = (gated_normed * ssm_norm_gain).astype(jnp.bfloat16)
    positions = start + jnp.arange(length, dtype=jnp.int32)
    cosine, sine = rope_tables(positions, HDIM)
    cosine = cosine[None, :, None, :]
    sine = sine[None, :, None, :]
    query = rotate(
        matmul(mixer_in, full_query_proj).reshape(batch, length, query_heads, HDIM),
        cosine,
        sine,
        1.0,
    ).astype(jnp.bfloat16)
    keys_new = rotate(
        matmul(mixer_in, full_key_proj).reshape(batch, length, key_heads, HDIM), cosine, sine, 1.0
    ).astype(jnp.bfloat16)
    values_new = matmul(mixer_in, full_attn_value).astype(jnp.bfloat16)
    kv_local = jnp.concatenate(
        [keys_new.reshape(batch, length, key_heads * HDIM), values_new], axis=-1
    )
    key_value_rows = lax.all_gather(kv_local, "seq", axis=1, tiled=True)
    query_group = query.reshape(batch, length, key_heads, group, HDIM)
    query_doc = lax.dynamic_slice_in_dim(doc_ids, start, length, 1)
    block = key_block()
    block_count = (start + length - 1) // block + 1

    def stats_step(index, carry):
        peak, total = carry
        scores, allowed, _, _ = block_scores(
            query_group, key_value_rows, index * block, block, doc_ids, positions, query_doc
        )
        masked = jnp.where(allowed, scores, NEG_LARGE)
        new_peak = jnp.maximum(peak, jnp.max(masked, axis=-1))
        total = total * jnp.exp(peak - new_peak) + jnp.sum(
            jnp.where(allowed, jnp.exp(masked - new_peak[..., None]), 0.0), axis=-1
        )
        return (new_peak, total)

    stat_shape = (batch, key_heads, group, length)
    peak, total = lax.fori_loop(
        0,
        block_count,
        stats_step,
        (jnp.full(stat_shape, NEG_LARGE, jnp.float32), jnp.zeros(stat_shape, jnp.float32)),
    )
    log_total = peak + jnp.log(total)

    def value_step(index, accum):
        scores, allowed, _, values = block_scores(
            query_group, key_value_rows, index * block, block, doc_ids, positions, query_doc
        )
        probs = jnp.where(allowed, jnp.exp(scores - log_total[..., None]), 0.0).astype(jnp.bfloat16)
        return accum + jnp.einsum(
            "scgqk,skcd->sqcgd", probs, values, preferred_element_type=jnp.float32
        )

    attn_out = lax.fori_loop(0, block_count, value_step, jnp.zeros(query_group.shape, jnp.float32))
    attn_in = attn_out.reshape(batch, length, query_heads * HDIM).astype(jnp.bfloat16)
    mixed = resid + head_sum(matmul(ssm_in, full_ssm_out) + matmul(attn_in, full_attn_out))
    normed_ffn, scale_ffn, scaled_ffn = rms_apply(mixed, full_ffn_gain)
    feedforward_input = scaled_ffn.astype(jnp.bfloat16)
    gate = matmul(feedforward_input, full_ffn_gate)
    upward = matmul(feedforward_input, full_ffn_up)
    sigma = jax.nn.sigmoid(gate)
    hidden_act = (gate * sigma * upward).astype(jnp.bfloat16)
    block_out = (mixed + head_sum(matmul(hidden_act, full_ffn_down))).astype(jnp.bfloat16)
    fetched = (
        lax.all_gather(mixer_gain, ("dp", "seq"), axis=0, tiled=True),
        lax.all_gather(ssm_gate_proj, ("dp", "seq"), axis=0, tiled=True),
        lax.all_gather(ssm_value_proj, ("dp", "seq"), axis=0, tiled=True),
        lax.all_gather(ssm_bc_proj, ("dp", "seq"), axis=0, tiled=True),
        lax.all_gather(ssm_step_proj, ("dp", "seq"), axis=0, tiled=True),
        lax.all_gather(query_proj, ("dp", "seq"), axis=0, tiled=True),
        lax.all_gather(key_proj, ("dp", "seq"), axis=0, tiled=True),
        lax.all_gather(value_proj, ("dp", "seq"), axis=0, tiled=True),
        lax.all_gather(ffn_gain, ("dp", "seq"), axis=0, tiled=True),
        lax.all_gather(ffn_gate_proj, ("dp", "seq"), axis=0, tiled=True),
        lax.all_gather(ffn_up_proj, ("dp", "seq"), axis=0, tiled=True),
        lax.all_gather(ssm_out_proj, ("dp", "seq"), axis=1, tiled=True),
        lax.all_gather(attn_out_proj, ("dp", "seq"), axis=1, tiled=True),
        lax.all_gather(ffn_down_proj, ("dp", "seq"), axis=1, tiled=True),
    )
    (
        full_mixer_gain,
        full_gate_proj,
        full_value_proj,
        full_bc_proj,
        full_step_proj,
        full_query_proj,
        full_key_proj,
        full_attn_value,
        full_ffn_gain,
        full_ffn_gate,
        full_ffn_up,
        full_ssm_out,
        full_attn_out,
        full_ffn_down,
    ) = fetched
    grad_top = out_grad.astype(jnp.float32)
    grad_ffn_down = weight_grad(hidden_act, out_grad)
    grad_hidden = back_product(out_grad, full_ffn_down)
    grad_gate_pre = (grad_hidden * upward * sigma * (1.0 + gate * (1.0 - sigma))).astype(
        jnp.bfloat16
    )
    grad_up_pre = (grad_hidden * gate * sigma).astype(jnp.bfloat16)
    grad_ffn_gate = weight_grad(feedforward_input, grad_gate_pre)
    grad_ffn_up = weight_grad(feedforward_input, grad_up_pre)
    grad_ffn_in = head_sum(
        back_product(grad_gate_pre, full_ffn_gate) + back_product(grad_up_pre, full_ffn_up)
    )
    grad_mixed_norm, grad_ffn_gain = rms_backward(grad_ffn_in, normed_ffn, scale_ffn, full_ffn_gain)
    grad_mixed = grad_top + grad_mixed_norm
    branch_gradient = grad_mixed.astype(jnp.bfloat16)
    grad_ssm_out = weight_grad(ssm_in, branch_gradient)
    grad_attn_out = weight_grad(attn_in, branch_gradient)
    grad_ssm = back_product(branch_gradient, full_ssm_out)
    grad_attn = back_product(branch_gradient, full_attn_out).reshape(
        batch, length, key_heads, group, HDIM
    )
    delta = jnp.transpose(jnp.sum(grad_attn * attn_out, axis=-1), (0, 2, 3, 1))
    grad_round = grad_attn.astype(jnp.bfloat16)

    def back_step(index, carry):
        grad_query, grad_kv = carry
        block_start = index * block
        scores, allowed, keys, values = block_scores(
            query_group, key_value_rows, block_start, block, doc_ids, positions, query_doc
        )
        probs = jnp.where(allowed, jnp.exp(scores - log_total[..., None]), 0.0)
        grad_values = jnp.einsum(
            "scgqk,sqcgd->skcd",
            probs.astype(jnp.bfloat16),
            grad_round,
            preferred_element_type=jnp.float32,
        )
        grad_probs = jnp.einsum(
            "sqcgd,skcd->scgqk", grad_round, values, preferred_element_type=jnp.float32
        )
        score_gradients = (probs * (grad_probs - delta[..., None]) * HDIM ** (-0.5)).astype(
            jnp.bfloat16
        )
        grad_query = grad_query + jnp.einsum(
            "scgqk,skcd->sqcgd", score_gradients, keys, preferred_element_type=jnp.float32
        )
        grad_keys = jnp.einsum(
            "scgqk,sqcgd->skcd", score_gradients, query_group, preferred_element_type=jnp.float32
        )
        piece = jnp.concatenate(
            [
                grad_keys.reshape(batch, block, key_heads * HDIM),
                grad_values.reshape(batch, block, key_heads * HDIM),
            ],
            axis=-1,
        )
        return (grad_query, lax.dynamic_update_slice_in_dim(grad_kv, piece, block_start, 1))

    grad_query, grad_kv = lax.fori_loop(
        0,
        block_count,
        back_step,
        (jnp.zeros(query_group.shape, jnp.float32), jnp.zeros(key_value_rows.shape, jnp.float32)),
    )
    grad_kv_own = lax.psum_scatter(grad_kv, "seq", scatter_dimension=1, tiled=True)
    grad_query_in = (
        rotate(grad_query.reshape(batch, length, query_heads, HDIM), cosine, sine, -1.0)
        .reshape(batch, length, query_heads * HDIM)
        .astype(jnp.bfloat16)
    )
    grad_key_in = (
        rotate(
            grad_kv_own[..., : key_heads * HDIM].reshape(batch, length, key_heads, HDIM),
            cosine,
            sine,
            -1.0,
        )
        .reshape(batch, length, key_heads * HDIM)
        .astype(jnp.bfloat16)
    )
    grad_value_in = grad_kv_own[..., key_heads * HDIM :].astype(jnp.bfloat16)
    grad_norm_gain = jnp.sum(grad_ssm * gated_normed, axis=(0, 1))
    scaled_grad = grad_ssm * ssm_norm_gain
    inner = norm_share(jnp.sum(scaled_grad * gated_normed, axis=-1))
    grad_gated = norm_scale * (scaled_grad - gated_normed * (inner[..., None] / inner_width))
    (
        grad_act_value,
        grad_act_bc,
        grad_step,
        grad_log_decay,
        grad_gate_raw,
        grad_state_in,
        grad_skip,
    ) = gated_pull(grad_gated)
    suffix = prefix_2(
        (decay, grad_state_in),
        "seq",
        combine_states,
        (jnp.ones_like(decay), jnp.zeros_like(grad_state_in)),
        True,
    )
    grad_ends = suffix[1]
    grad_decay = jnp.sum(grad_ends * state_in, axis=(2, 3))
    extra_value, extra_bc, extra_step, extra_log = ends_pull((grad_ends, grad_decay))
    (
        grad_value_ext,
        grad_step_raw,
        grad_kernel_value,
        grad_bias_value,
        grad_decay_log,
        grad_step_bias,
    ) = value_pull(
        (grad_act_value + extra_value, grad_step + extra_step, grad_log_decay + extra_log)
    )
    grad_bc_ext, grad_kernel_bc, grad_bias_bc = bc_pull(head_sum(grad_act_bc + extra_bc))
    boundary_gradients = passed_along(
        (grad_value_ext[:, :conv_width], grad_bc_ext[:, :conv_width]), "seq", -1
    )
    grad_value_raw = (
        grad_value_ext[:, conv_width:].at[:, length - conv_width :].add(boundary_gradients[0])
    )
    grad_bc_raw = (
        grad_bc_ext[:, conv_width:].at[:, length - conv_width :].add(boundary_gradients[1])
    )
    grad_gate_in = grad_gate_raw.astype(jnp.bfloat16)
    grad_value_ssm = grad_value_raw.astype(jnp.bfloat16)
    grad_bc_in = grad_bc_raw.astype(jnp.bfloat16)
    grad_step_in = grad_step_raw.astype(jnp.bfloat16)
    partial_sum = (
        back_product(grad_gate_in, full_gate_proj)
        + back_product(grad_value_ssm, full_value_proj)
        + back_product(grad_step_in, full_step_proj)
        + back_product(grad_query_in, full_query_proj)
        + back_product(grad_key_in, full_key_proj)
        + back_product(grad_value_in, full_attn_value)
    )
    grad_mixer_in = head_sum(partial_sum) + back_product(grad_bc_in, full_bc_proj)
    grad_pre_norm, grad_mixer_gain = rms_backward(
        grad_mixer_in, normed_pre, scale_pre, full_mixer_gain
    )
    hidden_grad = grad_mixed + grad_pre_norm
    reduced = (
        lax.psum_scatter(grad_mixer_gain, ("dp", "seq"), scatter_dimension=0, tiled=True),
        lax.psum_scatter(
            weight_grad(mixer_in, grad_gate_in), ("dp", "seq"), scatter_dimension=0, tiled=True
        ),
        lax.psum_scatter(
            weight_grad(mixer_in, grad_value_ssm), ("dp", "seq"), scatter_dimension=0, tiled=True
        ),
        lax.psum_scatter(
            weight_grad(mixer_in, grad_bc_in), ("dp", "seq"), scatter_dimension=0, tiled=True
        ),
        lax.psum_scatter(
            weight_grad(mixer_in, grad_step_in), ("dp", "seq"), scatter_dimension=0, tiled=True
        ),
        lax.psum_scatter(
            weight_grad(mixer_in, grad_query_in), ("dp", "seq"), scatter_dimension=0, tiled=True
        ),
        lax.psum_scatter(
            weight_grad(mixer_in, grad_key_in), ("dp", "seq"), scatter_dimension=0, tiled=True
        ),
        lax.psum_scatter(
            weight_grad(mixer_in, grad_value_in), ("dp", "seq"), scatter_dimension=0, tiled=True
        ),
        lax.psum_scatter(grad_ffn_gain, ("dp", "seq"), scatter_dimension=0, tiled=True),
        lax.psum_scatter(grad_ffn_gate, ("dp", "seq"), scatter_dimension=0, tiled=True),
        lax.psum_scatter(grad_ffn_up, ("dp", "seq"), scatter_dimension=0, tiled=True),
        lax.psum_scatter(grad_ssm_out, ("dp", "seq"), scatter_dimension=1, tiled=True),
        lax.psum_scatter(grad_attn_out, ("dp", "seq"), scatter_dimension=1, tiled=True),
        lax.psum_scatter(grad_ffn_down, ("dp", "seq"), scatter_dimension=1, tiled=True),
    )
    small = lax.psum(
        (
            grad_kernel_value,
            grad_bias_value,
            grad_kernel_bc,
            grad_bias_bc,
            grad_decay_log,
            grad_step_bias,
            grad_skip,
            grad_norm_gain,
        ),
        ("dp", "seq"),
    )
    return (
        block_out,
        hidden_grad,
        reduced[0],
        reduced[1],
        reduced[2],
        reduced[3],
        reduced[4],
        small[0],
        small[1],
        small[2],
        small[3],
        small[4],
        small[5],
        small[6],
        small[7],
        reduced[11],
        reduced[5],
        reduced[6],
        reduced[7],
        reduced[12],
        reduced[8],
        reduced[9],
        reduced[10],
        reduced[13],
    )


ROWS = 128


def mm(left, right, on_left, on_right):
    return lax.dot_general(
        left, right, (((on_left,), (on_right,)), ((), ())), preferred_element_type=jnp.float32
    )


def exact_mm(mask, values, on_mask):
    total = None
    for _ in range(3):
        part = values.astype(jnp.bfloat16)
        values = values - part.astype(jnp.float32)
        term = mm(mask, part, on_mask, 0)
        total = term if total is None else total + term
    return total


def sigmoid(values):
    return 1.0 / (1.0 + jnp.exp(-values))


def local_call(body, out_shape, scratch, args):
    windowed = any(isinstance(arg, Window) for arg in args)

    def whole(arg):
        if not windowed:
            return pl.BlockSpec(memory_space=pltpu.VMEM)
        return pl.BlockSpec(arg.shape, lambda _: (0, 0))

    def spec(arg):
        if arg.ndim == 1:
            return pl.BlockSpec(memory_space=pltpu.SMEM)
        if isinstance(arg, Window):
            block = arg.block
            return pl.BlockSpec(arg.shape, lambda _: (0, block))
        return whole(arg)

    return pl.pallas_call(
        body,
        out_shape=out_shape,
        in_specs=[spec(arg) for arg in args],
        out_specs=[whole(out) for out in out_shape],
        scratch_shapes=scratch,
        grid=(1,) if windowed else (),
    )(*(arg.array if isinstance(arg, Window) else arg for arg in args))


def shape_of(rows, columns, dtype=jnp.float32):
    return jax.ShapeDtypeStruct((rows, columns), dtype)


class Layout:
    def __init__(self, tokens, width, inner, nstate, kv, heads, taps, inner_width):
        self.tokens, self.width, self.inner, self.nstate = (tokens, width, inner, nstate)
        self.kv, self.heads, self.taps, self.inner_width = (kv, heads, taps, inner_width)
        self.hdim = inner // heads
        self.value = 2 * nstate
        self.attn_value = self.value + inner
        self.gate = self.attn_value + kv
        self.step = self.gate + inner
        self.gain = self.step + heads
        self.query = -(-(self.gain + 2) // 128) * 128
        self.total = self.query + 2 * kv
        self.step_tile = self.step // 128 * 128
        self.step_lane = self.step - self.step_tile


def put_pieces(target, pieces, head, half):
    count = len(pieces) // 2
    for j in range(count):
        own = pl.multiple_of((2 * j + head) * half, half)
        other = pl.multiple_of((2 * j + 1 - head) * half, half)
        target[pl.ds(own, half), :] = pieces[j][...]
        target[pl.ds(other, half), :] = pieces[count + j][...]


def split_product(left, weights, sent, mine, head, half):
    seqs = left.shape[0] // (2 * half)

    def rows_of(side):
        starts = [pl.multiple_of((2 * j + side) * half, half) for j in range(seqs)]
        return jnp.concatenate([left[pl.ds(start, half), :] for start in starts], axis=0)

    theirs, own = (rows_of(1 - head), rows_of(head))
    at = 0
    for weight in weights:
        columns = slice(at, at + weight.shape[0])
        at += weight.shape[0]
        sent[:, columns] = mm(theirs, weight[...], 1, 1).astype(sent.dtype)
        mine[:, columns] = mm(own, weight[...], 1, 1)


def times_pieces(left, weights):
    total, at = (None, 0)
    for weight in weights:
        size = weight.shape[0]
        term = mm(left[:, at : at + size], weight[...], 1, 0)
        total = term if total is None else total + term
        at += size
    return total


class Window:
    def __init__(self, array, first, width):
        self.array, self.block, self.shape = (array, first // width, (array.shape[0], width))
        self.ndim = 2


def window(array, first, width):
    if first % width == 0 and width % 128 == 0:
        return Window(array, first, width)
    return array[:, first : first + width]


def allowed_rows(meta, meta_column, start):
    column = meta_column[pl.ds(start, ROWS), :]
    return (column[:, 0:1] >= meta[0:1, :]) & (column[:, 1:2] == meta[1:2, :])


def conv_tile(raw, params, column, at, taps):
    source = raw[:, at : at + 128]
    pre = params[taps : taps + 1, at : at + 128]
    for k in range(taps):
        shift = taps - 1 - k
        moved = pltpu.roll(source, shift, 0) if shift else source
        pre = pre + params[k : k + 1, at : at + 128] * moved * column[:, 2 + k : 3 + k]
    return (source, pre)


def over_channels(lay, values):
    lanes = lax.broadcasted_iota(jnp.int32, (lay.tokens, lay.inner), 1)
    spread = values[:, lay.step_lane : lay.step_lane + 1]
    for j in range(1, lay.heads):
        own = values[:, lay.step_lane + j : lay.step_lane + j + 1]
        spread = jnp.where(lanes >= j * lay.hdim, own, spread)
    return spread


def head_lanes(lay, block, j):
    lanes = lax.broadcasted_iota(jnp.int32, block.shape, 1)
    kept = (lanes >= j * lay.hdim) & (lanes < (j + 1) * lay.hdim)
    return jnp.where(kept, block, jnp.zeros_like(block))


def head_selector(lay):
    channel = lax.broadcasted_iota(jnp.int32, (lay.inner, 128), 0)
    lane = lax.broadcasted_iota(jnp.int32, (lay.inner, 128), 1) - lay.step_lane
    inside = (channel >= lane * lay.hdim) & (channel < (lane + 1) * lay.hdim)
    return inside.astype(jnp.float32)


def row_sums(values):
    return lax.dot_general(
        jnp.ones((8, values.shape[1]), jnp.float32),
        values,
        (((1,), (1,)), ((), ())),
        precision=HIGH,
        preferred_element_type=jnp.float32,
    )


def mixer_forward(lay, pieces, weights, params, meta, head):
    count, parts = (len(pieces), len(weights))
    half = pieces[0].shape[0]
    chunk = lay.width // parts

    def body(*refs):
        piece_refs, weight_refs = (refs[:count], refs[count : count + parts])
        params, meta, head = refs[count + parts : count + parts + 3]
        (mixer_in, raw, cumul, intra, gated, squares, gains) = refs[count + parts + 3 : -4]
        hidden, act, stepped, column = refs[-4:]
        put_pieces(hidden, piece_refs, head[0], half)
        column[...] = meta[...].T
        tile = lay.gain // 128 * 128
        row = lay.gain - tile
        for k in range(parts):
            turned = weight_refs[k][:, tile : tile + 128].astype(jnp.float32).T
            gains[0:8, k * chunk : (k + 1) * chunk] = jnp.concatenate(
                [turned[row : row + 2], jnp.zeros((6, chunk), jnp.float32)], axis=0
            )

        def project(at, carry):
            start = pl.multiple_of(at * ROWS, ROWS)
            block = hidden[pl.ds(start, ROWS), :].astype(jnp.float32)
            scale = lax.rsqrt(jnp.mean(block * block, axis=-1, keepdims=True) + EPS)
            block = (block * scale * gains[0:1, :]).astype(jnp.bfloat16)
            mixer_in[pl.ds(start, ROWS), :] = block
            raw[pl.ds(start, ROWS), :] = times_pieces(block, weight_refs)
            return carry

        lax.fori_loop(0, lay.tokens // ROWS, project, 0)
        masks = column[...]
        for at in range(0, lay.gate, 128):
            _, pre = conv_tile(raw, params, masks, at, lay.taps)
            act[:, at : at + 128] = pre * sigmoid(pre)
        tile = slice(lay.step_tile, lay.step_tile + 128)
        step_pre = raw[:, tile] + params[lay.taps + 3 : lay.taps + 4, tile]
        step = jnp.maximum(step_pre, 0.0) + jnp.log1p(jnp.exp(-jnp.abs(step_pre)))
        log_decay = -step * params[lay.taps + 4 : lay.taps + 5, tile]
        value = act[:, lay.value : lay.value + lay.inner]
        stepped[...] = (value * over_channels(lay, step)).astype(jnp.bfloat16)

        def sums(at, carry):
            start = pl.multiple_of(at * ROWS, ROWS)
            mask = allowed_rows(meta, column, start).astype(jnp.bfloat16)
            cumul[pl.ds(start, ROWS), :] = exact_mm(mask, log_decay, 1)
            return carry

        lax.fori_loop(0, lay.tokens // ROWS, sums, 0)
        cumul_row = cumul[...].T
        input_b = act[:, : lay.nstate].astype(jnp.bfloat16)

        def mix(at, carry):
            start = pl.multiple_of(at * ROWS, ROWS)
            allowed = allowed_rows(meta, column, start)
            readout = act[pl.ds(start, ROWS), lay.nstate : 2 * lay.nstate].astype(jnp.bfloat16)
            cross = mm(readout, input_b, 1, 1)
            own = cumul[pl.ds(start, ROWS), :]
            total = None
            for j in range(lay.heads):
                lane = lay.step_lane + j
                gap = own[:, lane : lane + 1] - cumul_row[lane : lane + 1, :]
                mixing = jnp.exp(jnp.where(allowed, gap, NEG_LARGE)) * cross
                term = mm(mixing.astype(jnp.bfloat16), head_lanes(lay, stepped[...], j), 1, 0)
                total = term if total is None else total + term
            intra[pl.ds(start, ROWS), :] = total
            return carry

        lax.fori_loop(0, lay.tokens // ROWS, mix, 0)
        skip = params[lay.taps + 1 : lay.taps + 2, lay.value : lay.value + lay.inner]
        gate = raw[:, lay.gate : lay.gate + lay.inner]
        out = (intra[...] + skip * value) * (gate * sigmoid(gate))
        gated[...] = out
        squares[...] = row_sums(out * out)

    tokens = lay.tokens
    return local_call(
        body,
        (
            shape_of(tokens, lay.width, jnp.bfloat16),
            shape_of(tokens, lay.total),
            shape_of(tokens, 128),
            shape_of(tokens, lay.inner),
            shape_of(tokens, lay.inner),
            shape_of(8, tokens),
            shape_of(8, lay.width),
        ),
        [
            pltpu.VMEM((tokens, lay.width), jnp.bfloat16),
            pltpu.VMEM((tokens, lay.gate), jnp.float32),
            pltpu.VMEM((tokens, lay.inner), jnp.bfloat16),
            pltpu.VMEM((tokens, 8), jnp.float32),
        ],
        (*pieces, *weights, params, meta, head),
    )


def turn_lanes(block, cosine, sine, sign):
    size = block.shape[1]
    lanes = lax.broadcasted_iota(jnp.int32, block.shape, 1)
    first = lanes % HDIM < HDIM // 2
    ahead = pltpu.roll(block, size - HDIM // 2, 1)
    behind = pltpu.roll(block, HDIM // 2, 1)
    return block * cosine + sign * jnp.where(first, -ahead, behind) * sine


def attention_forward(lay, raw, meta, cosine, sine):
    def body(raw, meta, cosine, sine, turned, packed, column):
        column[...] = meta[...].T
        rotated = turn_lanes(
            raw[:, lay.query : lay.query + 2 * lay.kv], cosine[...], sine[...], 1.0
        )
        turned[...] = rotated.astype(jnp.bfloat16)
        keys = turned[:, lay.kv :]
        values = raw[:, lay.attn_value : lay.attn_value + lay.kv].astype(jnp.bfloat16)

        def rows(at, carry):
            start = pl.multiple_of(at * ROWS, ROWS)
            allowed = allowed_rows(meta, column, start)
            query = turned[pl.ds(start, ROWS), : lay.kv]
            scores = mm(query, keys, 1, 1) * HDIM ** (-0.5)
            scores = jnp.where(allowed, scores, NEG_LARGE)
            peak = jnp.max(scores, axis=-1, keepdims=True)
            total = jnp.sum(jnp.exp(scores - peak), axis=-1, keepdims=True)
            log_total = peak + jnp.log(total)
            probs = jnp.exp(scores - log_total).astype(jnp.bfloat16)
            out = mm(probs, values, 1, 0)
            packed[pl.ds(start, ROWS), :] = jnp.concatenate(
                [out, jnp.broadcast_to(log_total, out.shape)], axis=-1
            )
            return carry

        lax.fori_loop(0, lay.tokens // ROWS, rows, 0)

    return local_call(
        body,
        (shape_of(lay.tokens, 2 * lay.kv, jnp.bfloat16), shape_of(lay.tokens, 2 * lay.kv)),
        [pltpu.VMEM((lay.tokens, 8), jnp.float32)],
        (raw, meta, cosine, sine),
    )


def branch_product(lay, gated, packed, squares, params, weights, head, half):
    def body(gated, packed, squares, params, head, *rest):
        weights, (branch_in, sent, mine) = (rest[:-3], rest[-3:])
        scale = lax.rsqrt(squares[...] / lay.inner_width + EPS).T[:, 0:1]
        gain = params[lay.taps + 2 : lay.taps + 3, lay.value : lay.value + lay.inner]
        ssm_in = gated[...] * scale * gain
        branch_in[...] = jnp.concatenate([ssm_in, packed[:, : lay.kv]], axis=-1).astype(
            jnp.bfloat16
        )
        split_product(branch_in, weights, sent, mine, head[0], half)

    rows = lay.tokens // 2
    return local_call(
        body,
        (
            shape_of(lay.tokens, lay.inner + lay.kv, jnp.bfloat16),
            shape_of(rows, lay.width, jnp.bfloat16),
            shape_of(rows, lay.width),
        ),
        [],
        (gated, packed, squares, params, head, *weights),
    )


def halves_product(left, weights, head, half):
    def body(left, head, *rest):
        weights, (sent, mine) = (rest[:-2], rest[-2:])
        split_product(left, weights, sent, mine, head[0], half)

    rows, width = (left.shape[0] // 2, sum(weight.shape[0] for weight in weights))
    return local_call(
        body,
        (shape_of(rows, width, jnp.bfloat16), shape_of(rows, width)),
        [],
        (left, head, *weights),
    )


def add_and_part(mine, got, half):
    count = mine.shape[0] // half

    def body(mine, got, *parts):
        for j in range(count):
            rows = slice(j * half, (j + 1) * half)
            total = mine[rows, :] + got[rows, :].astype(jnp.float32)
            parts[j][...] = total.astype(parts[j].dtype)

    width = mine.shape[1]
    return local_call(
        body,
        [shape_of(half, width)] + [shape_of(half, width, jnp.bfloat16)] * (count - 1),
        [],
        (mine, got),
    )


def exchange(sent, mine, half):
    own, *parts = add_and_part(mine, partner(sent), half)
    return [own] + [to_ahead(part, "seq", j + 1) for j, part in enumerate(parts)]


def added(parts):
    total = parts[0][...]
    for part in parts[1:]:
        total = total + part[...].astype(jnp.float32)
    return total


def normed_of(values):
    scale = lax.rsqrt(jnp.mean(values * values, axis=-1, keepdims=True) + EPS)
    return (values * scale, scale)


def mix_and_norm(parts, resid, gains):
    count = len(parts)

    def body(*refs):
        resid, gains, mixed, out = refs[count:]
        total = resid[...].astype(jnp.float32) + added(refs[:count])
        mixed[...] = total
        out[...] = (normed_of(total)[0] * gains[1:2, :]).astype(jnp.bfloat16)

    return local_call(
        body,
        (shape_of(*resid.shape), shape_of(*resid.shape, jnp.bfloat16)),
        [],
        (*parts, resid, gains),
    )


def norm_pull(parts, values, base, gains, row):
    count = len(parts)

    def body(*refs):
        values, base, gains, out, rounded, gain_row = refs[count:]
        gradient = added(refs[:count])
        normed, scale = normed_of(values[...].astype(jnp.float32))
        scaled = gradient * gains[row : row + 1, :]
        mean = jnp.mean(scaled * normed, axis=-1, keepdims=True)
        total = base[...].astype(jnp.float32) + scale * (scaled - normed * mean)
        out[...] = total
        rounded[...] = total.astype(jnp.bfloat16)
        sums = jnp.sum(gradient * normed, axis=0, keepdims=True)
        gain_row[...] = jnp.broadcast_to(sums, gain_row.shape)

    return local_call(
        body,
        (
            shape_of(*values.shape),
            shape_of(*values.shape, jnp.bfloat16),
            shape_of(8, values.shape[1]),
        ),
        [],
        (*parts, values, base, gains),
    )


def feed_forward(pieces, up_pieces, weights_ffn, weights_down, head):
    count, parts = (len(pieces), len(weights_ffn))
    half, width = pieces[0].shape
    tokens, units = (half * count, weights_down[0].shape[1])

    def body(*refs):
        weights_ffn = refs[2 * count : 2 * count + parts]
        weights_down = refs[2 * count + parts : 2 * count + 2 * parts]
        head = refs[2 * count + 2 * parts]
        ffn_in, upstream, hidden_act, gradient, sent, mine = refs[-6:]
        put_pieces(ffn_in, refs[:count], head[0], half)
        put_pieces(upstream, refs[count : 2 * count], head[0], half)

        def rows(at, carry):
            start = pl.multiple_of(at * ROWS, ROWS)
            both = times_pieces(ffn_in[pl.ds(start, ROWS), :], weights_ffn)
            gate, upward = (both[:, :units], both[:, units:])
            sigma = sigmoid(gate)
            act = gate * sigma
            hidden_act[pl.ds(start, ROWS), :] = (act * upward).astype(jnp.bfloat16)
            pulled = times_pieces(upstream[pl.ds(start, ROWS), :], weights_down)
            gradient[pl.ds(start, ROWS), :] = jnp.concatenate(
                [pulled * upward * sigma * (1.0 + gate * (1.0 - sigma)), pulled * act], axis=-1
            ).astype(jnp.bfloat16)
            return carry

        lax.fori_loop(0, tokens // ROWS, rows, 0)
        split_product(gradient, weights_ffn, sent, mine, head[0], half)

    return local_call(
        body,
        (
            shape_of(tokens, width, jnp.bfloat16),
            shape_of(tokens, width, jnp.bfloat16),
            shape_of(tokens, units, jnp.bfloat16),
            shape_of(tokens, 2 * units, jnp.bfloat16),
            shape_of(tokens // 2, width, jnp.bfloat16),
            shape_of(tokens // 2, width),
        ),
        [],
        (*pieces, *up_pieces, *weights_ffn, *weights_down, head),
    )


def branch_backward(lay, pieces, weights, gated, squares, params, head):
    count = len(pieces)
    half = pieces[0].shape[0]

    def body(*refs):
        gated, squares, params, head = refs[count : count + 4]
        weights, (branch, gradient, overlap) = (refs[count + 4 : -3], refs[-3:])
        put_pieces(branch, refs[:count], head[0], half)
        gradient[...] = times_pieces(branch[...], weights)
        scale = lax.rsqrt(squares[...] / lay.inner_width + EPS).T[:, 0:1]
        gain = params[lay.taps + 2 : lay.taps + 3, lay.value : lay.value + lay.inner]
        overlap[...] = row_sums(gradient[:, : lay.inner] * gain * (gated[...] * scale))

    return local_call(
        body,
        (
            shape_of(lay.tokens, lay.width, jnp.bfloat16),
            shape_of(lay.tokens, lay.inner + lay.kv),
            shape_of(8, lay.tokens),
        ),
        [],
        (*pieces, gated, squares, params, head, *weights),
    )


def attention_backward(lay, gradient, raw, turned, packed, meta, cosine, sine):
    def body(
        gradient, raw, turned, packed, meta, cosine, sine, grad_turned, grad_values, column, pulls
    ):
        column[...] = meta[...].T
        keys = turned[:, lay.kv :]
        values = raw[:, lay.attn_value : lay.attn_value + lay.kv].astype(jnp.bfloat16)
        pulls[...] = jnp.zeros_like(pulls)
        grad_values[...] = jnp.zeros_like(grad_values)

        def rows(at, carry):
            start = pl.multiple_of(at * ROWS, ROWS)
            allowed = allowed_rows(meta, column, start)
            query = turned[pl.ds(start, ROWS), : lay.kv]
            saved = packed[pl.ds(start, ROWS), :]
            pulled = gradient[pl.ds(start, ROWS), lay.inner :]
            delta = jnp.sum(pulled * saved[:, : lay.kv], axis=-1, keepdims=True)
            pulled = pulled.astype(jnp.bfloat16)
            scores = mm(query, keys, 1, 1) * HDIM ** (-0.5)
            scores = jnp.where(allowed, scores, NEG_LARGE)
            probs = jnp.exp(scores - saved[:, lay.kv : lay.kv + 1])
            grad_values[...] += mm(probs.astype(jnp.bfloat16), pulled, 0, 0)
            grad_probs = mm(pulled, values, 1, 1)
            grad_scores = (probs * (grad_probs - delta) * HDIM ** (-0.5)).astype(jnp.bfloat16)
            pulls[pl.ds(start, ROWS), : lay.kv] = mm(grad_scores, keys, 1, 0)
            pulls[:, lay.kv :] += mm(grad_scores, query, 0, 0)
            return carry

        lax.fori_loop(0, lay.tokens // ROWS, rows, 0)
        grad_turned[...] = turn_lanes(pulls[...], cosine[...], sine[...], -1.0)

    return local_call(
        body,
        (shape_of(lay.tokens, 2 * lay.kv), shape_of(lay.tokens, lay.kv)),
        [
            pltpu.VMEM((lay.tokens, 8), jnp.float32),
            pltpu.VMEM((lay.tokens, 2 * lay.kv), jnp.float32),
        ],
        (gradient, raw, turned, packed, meta, cosine, sine),
    )


def mixer_backward(
    lay, gradient, raw, cumul, intra, squares, overlap, params, meta, grad_turned, grad_values
):
    def body(
        gradient,
        raw,
        cumul,
        intra,
        squares,
        overlap,
        params,
        meta,
        grad_turned,
        grad_values,
        grad_raw,
        small,
        column,
        act,
        stepped,
        grad_y,
        grad_act,
        grad_stepped,
        grad_step,
    ):
        taps, inner = (lay.taps, lay.inner)
        channels = slice(lay.value, lay.value + inner)
        column[...] = meta[...].T
        masks = column[...]
        small[...] = jnp.zeros_like(small)
        for at in range(0, lay.gate, 128):
            _, pre = conv_tile(raw, params, masks, at, taps)
            act[:, at : at + 128] = pre * sigmoid(pre)
        tile = slice(lay.step_tile, lay.step_tile + 128)
        step_pre = raw[:, tile] + params[taps + 3 : taps + 4, tile]
        step = jnp.maximum(step_pre, 0.0) + jnp.log1p(jnp.exp(-jnp.abs(step_pre)))
        rate = params[taps + 4 : taps + 5, tile]
        stepped[...] = (act[:, channels] * over_channels(lay, step)).astype(jnp.bfloat16)
        scale = lax.rsqrt(squares[...] / lay.inner_width + EPS).T[:, 0:1]
        shared = (overlap[...] / lay.inner_width).T[:, 0:1]
        skip = params[taps + 1 : taps + 2, channels]
        gain = params[taps + 2 : taps + 3, channels]
        gate = raw[:, lay.gate : lay.gate + inner]
        gate_sigma = sigmoid(gate)
        value = act[:, channels]
        out = intra[...] + skip * value
        normed = out * gate * gate_sigma * scale
        pulled = gradient[:, :inner]
        small[taps + 2 : taps + 3, channels] = jnp.sum(pulled * normed, axis=0, keepdims=True)
        pulled = scale * (pulled * gain - normed * shared)
        grad_gate = pulled * out * gate_sigma * (1.0 + gate * (1.0 - gate_sigma))
        pulled = pulled * gate * gate_sigma
        small[taps + 1 : taps + 2, channels] = jnp.sum(pulled * value, axis=0, keepdims=True)
        grad_y[...] = pulled.astype(jnp.bfloat16)
        grad_act[:, channels] = skip * pulled
        grad_act[:, : lay.nstate] = jnp.zeros((lay.tokens, lay.nstate), jnp.float32)
        grad_stepped[...] = jnp.zeros_like(grad_stepped)
        cumul_row = cumul[...].T
        input_b = act[:, : lay.nstate].astype(jnp.bfloat16)

        def mix(at, carry):
            start = pl.multiple_of(at * ROWS, ROWS)
            rows = pl.ds(start, ROWS)
            allowed = allowed_rows(meta, column, start)
            readout = act[rows, lay.nstate : 2 * lay.nstate].astype(jnp.bfloat16)
            cross = mm(readout, input_b, 1, 1)
            own = cumul[rows, :]
            grad_cross, total = (None, None)
            for j in range(lay.heads):
                lane = lay.step_lane + j
                gap = own[:, lane : lane + 1] - cumul_row[lane : lane + 1, :]
                decay = jnp.exp(jnp.where(allowed, gap, NEG_LARGE))
                pulled = head_lanes(lay, grad_y[rows, :], j)
                term = mm((decay * cross).astype(jnp.bfloat16), pulled, 0, 0)
                total = term if total is None else total + term
                term = mm(pulled, stepped[...], 1, 1) * decay
                grad_cross = term if grad_cross is None else grad_cross + term
            grad_stepped[...] += total
            grad_cross = grad_cross.astype(jnp.bfloat16)
            grad_act[rows, lay.nstate : 2 * lay.nstate] = mm(grad_cross, input_b, 1, 0)
            grad_act[:, : lay.nstate] += mm(grad_cross, readout, 0, 0)
            return carry

        lax.fori_loop(0, lay.tokens // ROWS, mix, 0)
        selector = head_selector(lay)
        moved = grad_stepped[...]
        change = grad_y[...].astype(jnp.float32) * intra[...] - moved * stepped[...].astype(
            jnp.float32
        )
        grad_cumul = jnp.dot(change, selector, precision=HIGH, preferred_element_type=jnp.float32)
        value = act[:, channels]
        grad_step[...] = jnp.zeros_like(grad_step)
        pieces = []
        rest = grad_cumul
        for _ in range(3):
            pieces.append(rest.astype(jnp.bfloat16))
            rest = rest - pieces[-1].astype(jnp.float32)
        for at in range(0, lay.tokens, ROWS):
            mask = allowed_rows(meta, column, at).astype(jnp.bfloat16)
            for piece in pieces:
                grad_step[...] += mm(mask, piece[at : at + ROWS], 0, 0)
        grad_log_decay = grad_step[...]
        small[taps + 4 : taps + 5, tile] = jnp.sum(
            grad_log_decay * (-step * rate), axis=0, keepdims=True
        )
        from_value = jnp.dot(
            moved * value, selector, precision=HIGH, preferred_element_type=jnp.float32
        )
        grad_step_raw = (from_value - grad_log_decay * rate) * sigmoid(step_pre)
        small[taps + 3 : taps + 4, tile] = jnp.sum(grad_step_raw, axis=0, keepdims=True)
        grad_act[:, channels] += moved * over_channels(lay, step)
        for at in range(0, lay.gate, 128):
            cols = slice(at, at + 128)
            source, pre = conv_tile(raw, params, masks, at, taps)
            sigma = sigmoid(pre)
            pulled = grad_act[:, cols] * sigma * (1.0 + pre * (1.0 - sigma))
            if at + 128 > lay.attn_value:
                lanes = lax.broadcasted_iota(jnp.int32, pulled.shape, 1) + at
                pulled = jnp.where(lanes < lay.attn_value, pulled, 0.0)
            small[taps : taps + 1, cols] = jnp.sum(pulled, axis=0, keepdims=True)
            total = None
            for k in range(taps):
                shift = taps - 1 - k
                masked = pulled * masks[:, 2 + k : 3 + k]
                moved = pltpu.roll(source, shift, 0) if shift else source
                small[k : k + 1, cols] = jnp.sum(masked * moved, axis=0, keepdims=True)
                term = masked * params[k : k + 1, cols]
                term = pltpu.roll(term, lay.tokens - shift, 0) if shift else term
                total = term if total is None else total + term
            grad_raw[:, cols] = total.astype(jnp.bfloat16)
        grad_raw[:, lay.attn_value : lay.gate] = grad_values[...].astype(jnp.bfloat16)
        grad_raw[:, tile] = grad_step_raw.astype(jnp.bfloat16)
        grad_raw[:, lay.gate : lay.step] = grad_gate.astype(jnp.bfloat16)
        grad_raw[:, lay.query :] = grad_turned[...].astype(jnp.bfloat16)

    tokens = lay.tokens
    return local_call(
        body,
        (shape_of(tokens, lay.total, jnp.bfloat16), shape_of(16, lay.total)),
        [
            pltpu.VMEM((tokens, 8), jnp.float32),
            pltpu.VMEM((tokens, lay.gate), jnp.float32),
            pltpu.VMEM((tokens, lay.inner), jnp.bfloat16),
            pltpu.VMEM((tokens, lay.inner), jnp.bfloat16),
            pltpu.VMEM((tokens, lay.gate), jnp.float32),
            pltpu.VMEM((tokens, lay.inner), jnp.float32),
            pltpu.VMEM((tokens, 128), jnp.float32),
        ],
        (
            gradient,
            raw,
            cumul,
            intra,
            squares,
            overlap,
            params,
            meta,
            grad_turned,
            grad_values,
        ),
    )


def shift_pairs(count, step):
    return [(i, (i + step) % count) for i in range(count)]


def from_ahead(block, axis, step):
    count = lax.axis_size(axis)
    return lax.ppermute(block, axis, shift_pairs(count, -step % count))


def to_ahead(block, axis, step):
    return lax.ppermute(block, axis, shift_pairs(lax.axis_size(axis), step))


def partner(block):
    return to_ahead(block, "head", 1)


def wrap_slice(block, start, axis):
    size = block.shape[axis]
    return lax.dynamic_slice_in_dim(jnp.concatenate([block, block], axis=axis), start, size, axis)


def dot_bf(left, right, dims):
    return lax.dot_general(left, right, (dims, ((), ())), preferred_element_type=jnp.float32)


def after(values, others):
    return lax.optimization_barrier((values, others))[0]


def gather_pieces(half):
    seqs = lax.axis_size("seq")
    own = [half] + [from_ahead(half, "seq", j) for j in range(1, seqs)]
    return own + [partner(piece) for piece in own]


def sum_tokens(values):
    seqs = lax.axis_size("seq")
    values = values + partner(values)
    block = values.shape[1] // seqs
    total = values
    for j in range(1, seqs):
        total = total + jnp.roll(from_ahead(values, "seq", j), j * block, axis=1)
    return total


def both_halves(half, head_at):
    other = partner(half)
    return jnp.where(
        head_at == 0,
        jnp.concatenate([half, other], axis=0),
        jnp.concatenate([other, half], axis=0),
    )


def dp_pieces(own):
    return [own] + [from_ahead(own, "dp", k) for k in range(1, lax.axis_size("dp"))]


def collect_weight_grad(pairs, seq_at):
    count, seqs = (lax.axis_size("dp"), lax.axis_size("seq"))
    chunk = pairs[0][0].shape[1] // count
    total = None
    for k in list(range(1, count)) + [0]:
        part = jnp.concatenate(
            [
                dot_bf(activation[:, k * chunk : (k + 1) * chunk], gradient, ((0,), (0,)))
                for activation, gradient in pairs
            ],
            axis=-1,
        )
        if k:
            part = to_ahead(part.astype(jnp.bfloat16), "dp", k).astype(jnp.float32)
        total = part if total is None else total + part
    rows = total.astype(jnp.bfloat16).reshape(seqs, chunk // seqs, -1)
    found = []
    for j in range(seqs):
        piece = lax.dynamic_index_in_dim(rows, (seq_at - j) % seqs, 0, keepdims=False)
        found.append(from_ahead(piece, "seq", j) if j else piece)
    return wrap_slice(jnp.stack(found), (seqs - seq_at) % seqs, 0).astype(jnp.float32)


def laid_out(found, first, width):
    part = jnp.moveaxis(found[:, :, first : first + width], 0, 1)
    return part.reshape(part.shape[0], -1)


def sum_all(values):
    for axis in ("dp", "seq"):
        count = lax.axis_size(axis)
        step = 1
        while step < count:
            values = values + lax.ppermute(values, axis, [(i, i ^ step) for i in range(count)])
            step *= 2
    return values


def fits_whole_sequences(sizes, args):
    batch, length, width = args[0].shape
    dps, seqs, heads = sizes
    tokens, mheads, inner = (length * seqs, args[12].shape[0], args[4].shape[1])
    attn, kv, bc, units = (args[i].shape[1] for i in (17, 18, 6, 22))
    powers = all(size & (size - 1) == 0 for size in sizes)
    even = all(part % seqs == 0 for part in (mheads, inner, attn, units))
    if not (powers and even and heads == 2 and batch == 1 and tokens <= 1024):
        return False
    conv = bc + inner // seqs
    aligned = bc % 256 == 0 and (conv + kv) % 128 == 0 and (2 * kv) % 128 == 0
    blocks = tokens % ROWS == 0 and length % 32 == 0 and width % (128 * dps) == 0
    single = kv == HDIM and attn // seqs == HDIM
    lane = (conv + kv + inner // seqs) % 128 + mheads // seqs + 2
    return aligned and blocks and single and units % (128 * seqs) == 0 and lane <= 128


def whole_sequences(
    hidden_in,
    out_grad,
    doc_ids,
    mixer_gain,
    ssm_gate_proj,
    ssm_value_proj,
    ssm_bc_proj,
    ssm_step_proj,
    conv_value_kernel,
    conv_value_bias,
    conv_bc_kernel,
    conv_bc_bias,
    decay_log,
    step_bias,
    skip_gain,
    ssm_norm_gain,
    ssm_out_proj,
    query_proj,
    key_proj,
    value_proj,
    attn_out_proj,
    ffn_gain,
    ffn_gate_proj,
    ffn_up_proj,
    ffn_down_proj,
):
    bf16, f32 = (jnp.bfloat16, jnp.float32)
    dps, seqs, heads = (lax.axis_size(axis) for axis in ("dp", "seq", "head"))
    dp_at, seq_at, head_at = (lax.axis_index(axis) for axis in ("dp", "seq", "head"))
    _, length, width = hidden_in.shape
    tokens = length * seqs
    half = length // heads
    rows = ssm_gate_proj.shape[0]
    chunk = width // dps
    inner = ssm_gate_proj.shape[1] // seqs
    mheads = decay_log.shape[0] // seqs
    kv = key_proj.shape[1]
    bc = ssm_bc_proj.shape[1]
    units = ffn_gate_proj.shape[1] // seqs
    taps = conv_value_kernel.shape[0]
    lay = Layout(
        tokens, width, inner, bc // 2, kv, mheads, taps, inner * seqs * heads
    )
    head = jnp.reshape(head_at, (1,)).astype(jnp.int32)

    def rotated(block):
        return wrap_slice(block, dp_at * chunk, block.ndim - 1)

    def unrotated(block):
        return wrap_slice(block, (dps - dp_at) % dps * chunk, block.ndim - 1)

    def cut(block):
        return jnp.moveaxis(block.reshape(rows, seqs, -1), 1, 0)

    def same(block):
        return jnp.broadcast_to(block[None], (seqs,) + block.shape)

    def own_part(block):
        size = block.shape[-1] // seqs
        return lax.dynamic_slice_in_dim(block, seq_at * size, size, block.ndim - 1)

    def exchanged_rows(pieces):
        found = lax.all_to_all(pieces, "seq", 0, 0, tiled=True)
        return found.reshape(-1, found.shape[-1])

    first_rows = exchanged_rows(
        jnp.concatenate(
            [
                same(ssm_bc_proj),
                cut(ssm_value_proj),
                same(value_proj),
                cut(ssm_gate_proj),
                cut(ssm_step_proj),
                same(mixer_gain[:, None]),
                same(ffn_gain[:, None]),
                jnp.zeros((seqs, rows, lay.query - lay.gain - 2), bf16),
                cut(query_proj),
                same(key_proj),
            ],
            axis=-1,
        )
    )
    hidden_half = rotated(lax.dynamic_slice_in_dim(hidden_in[0], head_at * half, half, 0))
    hidden = gather_pieces(hidden_half)
    weight_in = dp_pieces(first_rows)
    second_rows = exchanged_rows(
        after(
            jnp.concatenate(
                [
                    cut(ffn_gate_proj),
                    cut(ffn_up_proj),
                    cut(ssm_out_proj.T),
                    cut(attn_out_proj.T),
                    cut(ffn_down_proj.T),
                ],
                axis=-1,
            ),
            first_rows,
        )
    )
    grad_half = after(
        rotated(lax.dynamic_slice_in_dim(out_grad[0], head_at * half, half, 0)), first_rows
    )
    upstream_pieces = gather_pieces(grad_half)
    weight_rest = dp_pieces(second_rows)
    branch_width = inner + kv
    weight_ffn = [window(piece, 0, 2 * units) for piece in weight_rest]
    weight_out = [window(piece, 2 * units, branch_width) for piece in weight_rest]
    weight_down = [window(piece, 2 * units + branch_width, units) for piece in weight_rest]

    order = jnp.arange(tokens, dtype=jnp.int32)
    positions = (order + seq_at * length) % tokens
    docs = wrap_slice(doc_ids[0], seq_at * length, 0)
    meta = [positions, docs]
    for k in range(taps):
        shift = taps - 1 - k
        meta.append((positions >= shift) & (jnp.roll(docs, shift) == docs))
    meta = jnp.stack([row.astype(f32) for row in meta] + [jnp.zeros((tokens,), f32)] * (6 - taps))
    cosine, sine = rope_tables(positions, HDIM)
    cosine = jnp.tile(cosine, (1, 2 * 2 * kv // HDIM))
    sine = jnp.tile(sine, (1, 2 * 2 * kv // HDIM))

    def placed_row(values, first):
        return jnp.pad(values, ((0, 0), (first, lay.total - first - values.shape[1])))

    params = jnp.concatenate(
        [
            placed_row(
                jnp.concatenate(
                    [
                        jnp.concatenate([conv_bc_kernel, own_part(conv_value_kernel)], axis=-1),
                        jnp.concatenate([conv_bc_bias, own_part(conv_value_bias)])[None],
                    ],
                    axis=0,
                ),
                0,
            ),
            placed_row(
                jnp.stack(
                    [jnp.repeat(own_part(skip_gain), lay.hdim), own_part(ssm_norm_gain)]
                ),
                lay.value,
            ),
            placed_row(
                jnp.stack([own_part(step_bias), jnp.exp(own_part(decay_log))]), lay.step
            ),
            jnp.zeros((11 - taps, lay.total), f32),
        ],
        axis=0,
    )

    mixer_in, raw, cumul, intra, gated, squares, gains = mixer_forward(
        lay, hidden, weight_in, params, meta, head
    )
    squares = sum_tokens(squares)
    turned, packed = attention_forward(lay, raw, meta, cosine, sine)
    branch_in, sent, mine = branch_product(
        lay, gated, packed, squares, params, weight_out, head, half
    )
    mixed, ffn_half = mix_and_norm(exchange(sent, mine, half), hidden_half, gains)
    ffn_in, upstream, hidden_act, grad_ffn, sent, mine = feed_forward(
        gather_pieces(ffn_half), upstream_pieces, weight_ffn, weight_down, head
    )
    parts = exchange(sent, mine, half)
    grad_mixed, branch_half, grad_ffn_gain = norm_pull(parts, mixed, grad_half, gains, 1)
    branch, grad_branch, overlap = branch_backward(
        lay, gather_pieces(branch_half), weight_out, gated, squares, params, head
    )
    overlap = sum_tokens(overlap)
    found_ffn = collect_weight_grad(
        after([(ffn_in, grad_ffn), (upstream, hidden_act)], parts[0]), seq_at
    )
    found_branch = collect_weight_grad([(branch, branch_in)], seq_at)
    grad_turned, grad_values = attention_backward(
        lay, grad_branch, raw, turned, packed, meta, cosine, sine
    )
    sent, mine = halves_product(after(hidden_act, grad_branch), weight_down, head, half)
    block_half = sum(
        part.astype(f32) for part in exchange(sent, mine, half)
    )
    block_half = (mixed + block_half).astype(bf16)
    block_out = unrotated(both_halves(block_half, head_at))[None]

    grad_raw, small = mixer_backward(
        lay,
        grad_branch,
        raw,
        cumul,
        intra,
        squares,
        overlap,
        params,
        meta,
        grad_turned,
        grad_values,
    )
    sent, mine = halves_product(grad_raw, weight_in, head, half)
    hidden_grad, _, grad_mixer_gain = norm_pull(
        exchange(sent, mine, half), hidden_half, grad_mixed, gains, 0
    )
    hidden_grad = unrotated(both_halves(hidden_grad, head_at))[None]
    found_in = collect_weight_grad([(mixer_in, grad_raw)], seq_at)

    def in_place(block):
        size = block.shape[1]
        return lax.dynamic_update_slice_in_dim(
            jnp.zeros((block.shape[0], size * seqs), f32), block, seq_at * size, 1
        )

    channel = in_place(small[: taps + 3, lay.value : lay.value + inner])
    per_head = in_place(small[taps + 3 : taps + 5, lay.step : lay.step + mheads])
    whole = small[: taps + 1, :bc]
    grad_gains = unrotated(jnp.concatenate([grad_mixer_gain[:1], grad_ffn_gain[:1]], axis=0))
    listed = [channel, per_head, whole, grad_gains]
    summed = sum_all(jnp.concatenate([part.reshape(-1) for part in listed]))
    at_whole = channel.size + per_head.size
    shared = summed[at_whole:]
    shared = shared + partner(shared)
    channel = summed[: channel.size].reshape(channel.shape)
    per_head = summed[channel.size : at_whole].reshape(per_head.shape)
    whole = shared[: whole.size].reshape(whole.shape)
    grad_gains = lax.dynamic_slice_in_dim(
        shared[whole.size :].reshape(grad_gains.shape), (dp_at * seqs + seq_at) * rows, rows, 1
    )
    over_seq = jnp.sum(found_in, axis=0)
    grad_bc_proj = over_seq[:, :bc]
    grad_bc_proj = grad_bc_proj + partner(grad_bc_proj)
    return (
        block_out,
        hidden_grad,
        grad_gains[0],
        laid_out(found_in, lay.gate, inner),
        laid_out(found_in, lay.value, inner),
        grad_bc_proj,
        laid_out(found_in, lay.step, mheads),
        channel[:taps],
        channel[taps],
        whole[:taps],
        whole[taps],
        per_head[1],
        per_head[0],
        jnp.sum(channel[taps + 1].reshape(-1, lay.hdim), axis=-1),
        channel[taps + 2],
        laid_out(found_branch, 0, inner).T,
        laid_out(found_in, lay.query, kv),
        over_seq[:, lay.query + kv :],
        over_seq[:, lay.attn_value : lay.gate],
        laid_out(found_branch, inner, kv).T,
        grad_gains[1],
        laid_out(found_ffn, 0, units),
        laid_out(found_ffn, units, units),
        laid_out(found_ffn, 2 * units, units).T,
    )


def block_step(*args):
    sizes = tuple(lax.axis_size(axis) for axis in ("dp", "seq", "head"))
    if fits_whole_sequences(sizes, args):
        return whole_sequences(*args)
    return local(*args)


def solution(mesh):
    placed = (
        P("dp", "seq", None),
        P("dp", "seq", None),
        P("dp", None),
        P(("dp", "seq")),
        P(("dp", "seq"), "head"),
        P(("dp", "seq"), "head"),
        P(("dp", "seq"), None),
        P(("dp", "seq"), "head"),
        P(None, "head"),
        P("head"),
        P(),
        P(),
        P("head"),
        P("head"),
        P("head"),
        P("head"),
        P("head", ("dp", "seq")),
        P(("dp", "seq"), "head"),
        P(("dp", "seq"), "head"),
        P(("dp", "seq"), "head"),
        P("head", ("dp", "seq")),
        P(("dp", "seq")),
        P(("dp", "seq"), "head"),
        P(("dp", "seq"), "head"),
        P("head", ("dp", "seq")),
    )
    return jax.shard_map(
        block_step,
        mesh=mesh,
        in_specs=placed,
        out_specs=(
            P("dp", "seq", None),
            P("dp", "seq", None),
            P(("dp", "seq")),
            P(("dp", "seq"), "head"),
            P(("dp", "seq"), "head"),
            P(("dp", "seq"), None),
            P(("dp", "seq"), "head"),
            P(None, "head"),
            P("head"),
            P(),
            P(),
            P("head"),
            P("head"),
            P("head"),
            P("head"),
            P("head", ("dp", "seq")),
            P(("dp", "seq"), "head"),
            P(("dp", "seq"), "head"),
            P(("dp", "seq"), "head"),
            P("head", ("dp", "seq")),
            P(("dp", "seq")),
            P(("dp", "seq"), "head"),
            P(("dp", "seq"), "head"),
            P("head", ("dp", "seq")),
        ),
        check_vma=False,
    )
```
